128 devices in a mesh: gx: 4 (over x_hi, core), gy: 4 (over z), gz: 8 (over y, x_lo).
Axes of the slice: x: 4 (x_hi: 2, x_lo: 2; x = x_hi * 2 + x_lo), y: 4, z: 4, core: 2. Of those that a mesh axis runs over, the one named last changes fastest.
Arguments:
- load_data: float32 [4, 4, 8, 128, 1536], P('gx', 'gy', 'gz'), may hold values from -6 to 6
- initial_dual: float32 [4, 4, 8, 128, 1536], P('gx', 'gy', 'gz'), may hold values from -6 to 6
- dual_operator: float32 [4, 4, 8, 1536, 1536], P('gx', 'gy', 'gz'), as said below
- coarse_modes: float32 [4, 4, 8, 64, 1536], P('gx', 'gy', 'gz'), may hold values from -0.15625 to 0.15625
- coarse_inverse: float32 [8192, 8192], P(('gx', 'gy', 'gz')), as said below
- face_start: int32 [4, 4, 8, 6], P('gx', 'gy', 'gz'), may hold values from 0 to 1535, as said below
- face_len: int32 [4, 4, 8, 6], P('gx', 'gy', 'gz'), may hold values from 128 to 256, as said below
- multiplicity: int32 [4, 4, 8, 1536], P('gx', 'gy', 'gz'), may hold values from 2 to 4
Outputs:
- dual_solution: float32 [4, 4, 8, 128, 1536], P('gx', 'gy', 'gz')
- final_residual: float32 [4, 4, 8, 128, 1536], P('gx', 'gy', 'gz')
The draws below stay inside these ranges and needn't reach their ends.
Inputs may be any that keep to these rules, and one draw needn't show every extreme that they name: `face_len`: on each subdomain the six face segments lie within 0 to 1535 and do not intersect; the pieces on the two faces that meet between neighbouring subdomains have the same length; some face between two subdomains has exactly 256 unknowns. `face_start`: start of each face segment; see face_len. `dual_operator`: each subdomain's block is symmetric. `coarse_inverse`: the matrix is symmetric.
All inputs are finite; a program needn't handle non-finite values.
Results may differ from the reference program's by a relative error of at most 0.0003.
Values sent between devices are 32-bit elements; how exact they have to be, the bound alone decides.
No kernel may reach another device: no remote copies, remote signals or barrier semaphores. Data moves between devices by JAX's collectives and lax.ppermute only.
A program may use at most 128 MiB of HBM per device.

```python
import jax
import jax.numpy as jnp
from jax import lax

M = 1536
PCAP = 256
NM = 64
LOADS = 128
OUTER = 2
CHEB = 3
SX = 4
SY = 4
SZ = 8
C = 8192


def face_layout(key):
    base = jax.random.fold_in(key, 7001)
    keys = jax.random.split(base, 6)
    lowest = PCAP // 2
    len_x = jax.random.randint(keys[0], (SX + 1, SY, SZ), lowest, PCAP + 1)
    len_y = jax.random.randint(keys[1], (SX, SY + 1, SZ), lowest, PCAP + 1)
    len_z = jax.random.randint(keys[2], (SX, SY, SZ + 1), lowest, PCAP + 1)
    chosen = jax.random.randint(keys[3], (), 0, (SX - 1) * SY * SZ) + SY * SZ
    len_x = len_x.reshape(-1).at[chosen].set(PCAP).reshape(SX + 1, SY, SZ)
    lengths = jnp.stack([len_x[:-1], len_x[1:], len_y[:, :-1], len_y[:, 1:], len_z[:, :, :-1], len_z[:, :, 1:]], axis=-1)
    scores = jax.random.randint(keys[4], (SX, SY, SZ, 6), 0, 1000) * 8 + jnp.arange(6, dtype=jnp.int32)
    placing = jnp.argsort(scores, axis=-1)
    ordered = jnp.take_along_axis(lengths, placing, axis=-1)
    slack = M - jnp.sum(lengths, axis=-1, keepdims=True)
    shares = jax.random.randint(keys[5], (SX, SY, SZ, 6), 1, 100)
    gaps = slack * shares // jnp.sum(shares, axis=-1, keepdims=True)
    starts_ordered = jnp.cumsum(gaps + ordered, axis=-1) - ordered
    inverse = jnp.argsort(placing, axis=-1)
    starts = jnp.take_along_axis(starts_ordered, inverse, axis=-1)
    return (starts.astype(jnp.int32), lengths.astype(jnp.int32))


def draw_face_start(key, part):
    return face_layout(key)[0]


def draw_face_len(key, part):
    return face_layout(key)[1]


def symmetric_matrix(key, leading, order, spread):
    keys = jax.random.split(jax.random.fold_in(key, 7002), 2)
    shape = leading + (order, order)
    diagonal = jnp.exp(jax.random.uniform(keys[0], leading + (order,), jnp.float32, jnp.log(0.5), jnp.log(1.5)))
    coupling = jax.random.normal(keys[1], shape, jnp.float32)
    coupling = (coupling + jnp.swapaxes(coupling, -1, -2)) * (spread / jnp.sqrt(2.0 * order))
    identity = jnp.eye(order, dtype=jnp.float32)
    return coupling + diagonal[..., None] * identity


def draw_dual_operator(key, part):
    return symmetric_matrix(key, (SX, SY, SZ), M, 0.25)


def draw_coarse_inverse(key, part):
    return symmetric_matrix(key, (), C, 0.3)


def place_ends(entries, stream_key, smallest, top_value):
    dims = entries.shape
    index_at = [jax.random.randint(jax.random.fold_in(stream_key, axis), (), 0, dims[axis]) for axis in range(len(dims))]
    entries = entries.at[tuple(index_at)].set(smallest)
    longest = dims.index(max(dims))
    index_at[longest] = (index_at[longest] + 1) % dims[longest]
    return entries.at[tuple(index_at)].set(top_value)


def block_scale(stream_key, shape, cuts, low, high):
    def one(position, blocks):
        draws = jax.random.uniform(jax.random.fold_in(jax.random.fold_in(stream_key, 6), position), (blocks,), jnp.float32, low / len(cuts), high / len(cuts))
        return jnp.repeat(jnp.exp(draws), shape[position] // blocks).reshape((-1,) + (1,) * (len(shape) - position - 1))

    gain = one(*cuts[0])
    for cut in cuts[1:]:
        gain = gain * one(*cut)
    return gain


def noise(stream_key, shape, scale, limit, shards=(), held_as=jnp.bfloat16):
    loudness = block_scale(stream_key, shape, shards, -0.22, 0.18) if shards else 1.0
    drawn = jax.random.normal(stream_key, shape, jnp.float32) * scale * loudness
    return jnp.minimum(jnp.maximum(drawn, -limit), limit).astype(held_as)


def setup_inputs(seed: int = 0) -> dict:
    key_list = jax.random.split(jax.random.key(seed), 9)
    load_data = noise(key_list[0], (SX, SY, SZ, LOADS, M), 1.0, 6.0, ((0, 4), (1, 4), (2, 8)), jnp.float32)
    initial_dual = noise(key_list[1], (SX, SY, SZ, LOADS, M), 1.0, 6.0, ((0, 4), (1, 4), (2, 8)), jnp.float32)
    dual_operator = draw_dual_operator(jax.random.fold_in(key_list[8], 71), 0)
    coarse_modes = noise(key_list[3], (SX, SY, SZ, NM, M), M ** -0.5, 0.15625, ((0, 4), (1, 4), (2, 8)), jnp.float32)
    coarse_inverse = draw_coarse_inverse(jax.random.fold_in(key_list[8], 71), 0)
    face_start = draw_face_start(jax.random.fold_in(key_list[8], 71), 0)
    face_len = draw_face_len(jax.random.fold_in(key_list[8], 71), 0)
    multiplicity = place_ends(jax.random.randint(key_list[7], (SX, SY, SZ, M), 2, 5), jax.random.fold_in(key_list[7], 1), 2, 4).astype(jnp.int32)
    return {"load_data": load_data, "initial_dual": initial_dual, "dual_operator": dual_operator, "coarse_modes": coarse_modes, "coarse_inverse": coarse_inverse, "face_start": face_start, "face_len": face_len, "multiplicity": multiplicity}


highest = lax.Precision.HIGHEST
center = 1.0
half_width = 0.9


def face_pieces(values, starts, lengths):
    padded = jnp.pad(values, ((0, 0), (0, PCAP)))
    offsets = jnp.arange(PCAP, dtype=jnp.int32)
    gathered = []
    for face_id in range(6):
        anchor = starts[face_id].astype(jnp.int32)
        segment = lax.dynamic_slice(padded, (jnp.int32(0), anchor), (values.shape[0], PCAP))
        gathered.append(jnp.where(offsets < lengths[face_id], segment, 0.0))
    return jnp.stack(gathered)


def place_pieces(values, received, starts, lengths):
    padded = jnp.pad(values, ((0, 0), (0, PCAP)))
    offsets = jnp.arange(PCAP, dtype=jnp.int32)
    for face_id in range(6):
        anchor = starts[face_id].astype(jnp.int32)
        window = lax.dynamic_slice(padded, (jnp.int32(0), anchor), (values.shape[0], PCAP))
        window = window + jnp.where(offsets < lengths[face_id], received[face_id], 0.0)
        padded = lax.dynamic_update_slice(padded, window, (jnp.int32(0), anchor))
    return padded[:, :values.shape[1]]


def from_lower(stacked, along):
    zeros_slab = jnp.zeros_like(lax.slice_in_dim(stacked, 0, 1, axis=along))
    return jnp.concatenate([zeros_slab, lax.slice_in_dim(stacked, 0, stacked.shape[along] - 1, axis=along)], along)


def from_upper(stacked, along):
    zeros_slab = jnp.zeros_like(lax.slice_in_dim(stacked, 0, 1, axis=along))
    return jnp.concatenate([lax.slice_in_dim(stacked, 1, stacked.shape[along], axis=along), zeros_slab], along)


def operate(vectors, operator, starts, lengths, inverse_weight):
    subdomains = SX * SY * SZ
    product = jnp.einsum('abckm,abcmn->abckn', vectors, operator, precision=highest)
    flat_product = product.reshape(subdomains, LOADS, M)
    flat_starts = starts.reshape(subdomains, 6)
    flat_lengths = lengths.reshape(subdomains, 6)
    pieces = jax.vmap(face_pieces)(flat_product, flat_starts, flat_lengths)
    pieces = pieces.reshape(SX, SY, SZ, 6, LOADS, PCAP)
    received = jnp.stack([
        from_lower(pieces[:, :, :, 1], 0), from_upper(pieces[:, :, :, 0], 0),
        from_lower(pieces[:, :, :, 3], 1), from_upper(pieces[:, :, :, 2], 1),
        from_lower(pieces[:, :, :, 5], 2), from_upper(pieces[:, :, :, 4], 2)], axis=3)
    received = received.reshape(subdomains, 6, LOADS, PCAP)
    summed = jax.vmap(place_pieces)(flat_product, received, flat_starts, flat_lengths)
    return summed.reshape(SX, SY, SZ, LOADS, M) * inverse_weight[:, :, :, None, :]


def project(vectors, coarse_modes, coarse_inverse):
    subdomains = SX * SY * SZ
    coeffs = jnp.einsum('abckm,abcjm->abckj', vectors, coarse_modes, precision=highest)
    coeff_all = coeffs.reshape(subdomains, LOADS, NM).transpose(1, 0, 2).reshape(LOADS, C)
    amplitude_all = lax.dot_general(coeff_all, coarse_inverse, (((1,), (1,)), ((), ())), precision=highest)
    amplitude = amplitude_all.reshape(LOADS, subdomains, NM).transpose(1, 0, 2).reshape(SX, SY, SZ, LOADS, NM)
    return vectors - jnp.einsum('abckj,abcjm->abckm', amplitude, coarse_modes, precision=highest)


def reference(load_data, initial_dual, dual_operator, coarse_modes, coarse_inverse, face_start, face_len, multiplicity):
    inverse_weight = 1.0 / multiplicity.astype(jnp.float32)
    multipliers = initial_dual
    for outer_idx in range(OUTER):
        residual = load_data - operate(multipliers, dual_operator, face_start, face_len, inverse_weight)
        stretch = center / half_width
        rho_now = 1.0 / stretch
        correction = residual / center
        for inner_idx in range(CHEB):
            multipliers = multipliers + correction
            if inner_idx < CHEB - 1:
                residual = residual - operate(correction, dual_operator, face_start, face_len, inverse_weight)
                rho_next = 1.0 / (2.0 * stretch - rho_now)
                correction = (rho_next * rho_now) * correction + (2.0 * rho_next / half_width) * residual
                rho_now = rho_next
        multipliers = project(multipliers, coarse_modes, coarse_inverse)
    final_residual = load_data - operate(multipliers, dual_operator, face_start, face_len, inverse_weight)
    return multipliers, final_residual
```

```python
import functools

import jax
import jax.numpy as jnp
from jax import lax
from jax.experimental import pallas as pl
from jax.experimental.pallas import tpu as pltpu
from jax.sharding import Mesh, PartitionSpec as P

M = 1536
PCAP = 256
NM = 64
LOADS = 128
OUTER = 2
CHEB = 3
CHUNK = 256
NCHUNK = M // CHUNK


center = 1.0
half_width = 0.9

f32 = jnp.float32
bf16 = jnp.bfloat16

GX = ("xh", "co")
GY = ("gy",)
GZ = ("y", "xl")
RSG = ("co", "gy")

VEC = jax.ShapeDtypeStruct((M, LOADS), f32)
PIECE = jax.ShapeDtypeStruct((PCAP, LOADS), f32)
COEF = jax.ShapeDtypeStruct((NM, LOADS), f32)
VMEM = pl.BlockSpec(memory_space=pltpu.VMEM)
SMEM = pl.BlockSpec(memory_space=pltpu.SMEM)
ANY = pl.BlockSpec(memory_space=pl.ANY)


def split(x):
    high = x.astype(bf16)
    return high, (x - high.astype(f32)).astype(bf16)


def side_by_side(x):
    return jnp.concatenate(split(x), axis=1)


def fold(x):
    return x[:, :LOADS] + x[:, LOADS:]


def dot(a, b):
    return lax.dot_general(a, b, (((1,), (0,)), ((), ())), preferred_element_type=f32)


def start_operator(high, low, high_buf, low_buf, sems):
    copies = []
    for k in range(NCHUNK):
        rows = pl.ds(k * CHUNK, CHUNK)
        pair = (
            pltpu.make_async_copy(high.at[rows], high_buf.at[rows], sems.at[0, k]),
            pltpu.make_async_copy(low.at[rows], low_buf.at[rows], sems.at[1, k]),
        )
        for copy in pair:
            copy.start()
        copies.append(pair)
    return copies


def apply_operator(copies, high_buf, low_buf, wide, padded):
    for k in range(NCHUNK):
        for copy in copies[k]:
            copy.wait()
        rows = pl.ds(k * CHUNK, CHUNK)
        both = dot(high_buf[rows, :], wide[...]) + dot(low_buf[rows, :], wide[...])
        padded[rows, :] = fold(both)
    padded[pl.ds(M, PCAP), :] = jnp.zeros((PCAP, LOADS), f32)


def cut(starts, padded, product, pieces):
    product[...] = padded[pl.ds(0, M), :]
    for face in range(6):
        pieces[face][...] = padded[pl.ds(starts[face], PCAP), :]


def place(starts, lengths, product, received, padded):
    padded[pl.ds(0, M), :] = product[...]
    row = lax.broadcasted_iota(jnp.int32, (PCAP, LOADS), 0)
    for face in range(6):
        window = pl.ds(starts[face], PCAP)
        padded[window, :] = padded[window, :] + jnp.where(
            row < lengths[face], received[face][...], 0.0
        )
    return padded[pl.ds(0, M), :]


OPERATOR_SCRATCH = [
    pltpu.VMEM((M, M), bf16),
    pltpu.VMEM((M, M), bf16),
    pltpu.VMEM((M, 2 * LOADS), bf16),
    pltpu.VMEM((M + PCAP, LOADS), f32),
    pltpu.SemaphoreType.DMA((2, NCHUNK)),
]


def params(megabytes):
    return pltpu.CompilerParams(vmem_limit_bytes=megabytes << 20)


def first_kernel(starts, operator, vectors, high, low, vectors_t, product, *rest):
    pieces, (wide, padded) = rest[:6], rest[6:]
    step = pl.program_id(0)

    @pl.when(step == 0)
    def _():
        turned = vectors[...].T
        vectors_t[...] = turned
        wide[...] = side_by_side(turned)
        padded[pl.ds(M, PCAP), :] = jnp.zeros((PCAP, LOADS), f32)

    block_high, block_low = split(operator[...])
    high[...] = block_high
    low[...] = block_low
    both = dot(block_high, wide[...]) + dot(block_low, wide[...])
    padded[pl.ds(pl.multiple_of(step * CHUNK, CHUNK), CHUNK), :] = fold(both)

    @pl.when(step == NCHUNK - 1)
    def _():
        cut(starts, padded, product, pieces)


def first_apply(starts, operator, vectors):
    rows = pl.BlockSpec((CHUNK, M), lambda i: (i, 0))
    whole = pl.BlockSpec((M, LOADS), lambda i: (0, 0))
    piece = pl.BlockSpec((PCAP, LOADS), lambda i: (0, 0))
    return pl.pallas_call(
        first_kernel,
        grid=(NCHUNK,),
        out_shape=[
            jax.ShapeDtypeStruct((M, M), bf16),
            jax.ShapeDtypeStruct((M, M), bf16),
            VEC,
            VEC,
        ]
        + [PIECE] * 6,
        in_specs=[SMEM, rows, pl.BlockSpec((LOADS, M), lambda i: (0, 0))],
        out_specs=[rows, rows, whole, whole] + [piece] * 6,
        scratch_shapes=[
            pltpu.VMEM((M, 2 * LOADS), bf16),
            pltpu.VMEM((M + PCAP, LOADS), f32),
        ],
        compiler_params=params(40),
        name="first",
    )(starts, operator, vectors)


def turn_kernel(data, weight, modes, data_t, weight_t, modes_rows, modes_t):
    data_t[...] = data[...].T
    weight_t[...] = jnp.broadcast_to((1.0 / weight[...].astype(f32)), (LOADS, M)).T
    high, low = split(modes[...])
    modes_rows[...] = jnp.concatenate([high, low], axis=0)
    high, low = split(modes[...].T)
    modes_t[...] = jnp.concatenate([high, low, high], axis=1)


def turn(data, weight, modes):
    return pl.pallas_call(
        turn_kernel,
        out_shape=[
            VEC,
            VEC,
            jax.ShapeDtypeStruct((2 * NM, M), bf16),
            jax.ShapeDtypeStruct((M, 3 * NM), bf16),
        ],
        in_specs=[VMEM] * 3,
        out_specs=[VMEM] * 4,
        compiler_params=params(20),
        name="turn",
    )(data, weight, modes)


def start_kernel(starts, lengths, high, low, product, weight, data, multipliers, *rest):
    received, outs, scratch = rest[:6], rest[6:16], rest[16:]
    residual, correction, new_multipliers, new_product = outs[:4]
    high_buf, low_buf, wide, padded, sems = scratch
    copies = start_operator(high, low, high_buf, low_buf, sems)
    applied = place(starts, lengths, product, received, padded) * weight[...]
    new_residual = data[...] - applied
    residual[...] = new_residual
    new_correction = new_residual / center
    correction[...] = new_correction
    new_multipliers[...] = multipliers[...] + new_correction
    wide[...] = side_by_side(new_correction)
    apply_operator(copies, high_buf, low_buf, wide, padded)
    cut(starts, padded, new_product, outs[4:])


def start_step(starts, lengths, high, low, product, weight, data, multipliers, received):
    return pl.pallas_call(
        start_kernel,
        out_shape=[VEC] * 4 + [PIECE] * 6,
        in_specs=[SMEM, SMEM, ANY, ANY] + [VMEM] * 10,
        out_specs=[VMEM] * 10,
        scratch_shapes=OPERATOR_SCRATCH,
        compiler_params=params(32),
        name="start",
    )(starts, lengths, high, low, product, weight, data, multipliers, *received)


def inner_kernel(
    scale, gain, starts, lengths, high, low, product, weight, residual, correction, multipliers, *rest
):
    received, outs, scratch = rest[:6], rest[6:16], rest[16:]
    new_residual, new_correction, new_multipliers, new_product = outs[:4]
    high_buf, low_buf, wide, padded, sems = scratch
    copies = start_operator(high, low, high_buf, low_buf, sems)
    applied = place(starts, lengths, product, received, padded) * weight[...]
    remaining = residual[...] - applied
    new_residual[...] = remaining
    step = scale * correction[...] + gain * remaining
    new_correction[...] = step
    new_multipliers[...] = multipliers[...] + step
    wide[...] = side_by_side(step)
    apply_operator(copies, high_buf, low_buf, wide, padded)
    cut(starts, padded, new_product, outs[4:])


def inner_step(
    scale, gain, starts, lengths, high, low, product, weight, residual, correction, multipliers, received
):
    return pl.pallas_call(
        functools.partial(inner_kernel, scale, gain),
        out_shape=[VEC] * 4 + [PIECE] * 6,
        in_specs=[SMEM, SMEM, ANY, ANY] + [VMEM] * 11,
        out_specs=[VMEM] * 10,
        scratch_shapes=OPERATOR_SCRATCH,
        compiler_params=params(32),
        name="inner",
    )(starts, lengths, high, low, product, weight, residual, correction, multipliers, *received)


def last_kernel(
    scale, gain, starts, lengths, modes, product, weight, residual, correction, multipliers, *rest
):
    received, (new_multipliers, coeffs, padded) = rest[:6], rest[6:]
    applied = place(starts, lengths, product, received, padded) * weight[...]
    remaining = residual[...] - applied
    step = scale * correction[...] + gain * remaining
    moved = multipliers[...] + step
    new_multipliers[...] = moved
    both = dot(modes[...], side_by_side(moved))
    coeffs[...] = fold(both[:NM] + both[NM:])


def last_step(
    scale, gain, starts, lengths, modes, product, weight, residual, correction, multipliers, received
):
    return pl.pallas_call(
        functools.partial(last_kernel, scale, gain),
        out_shape=[VEC, COEF],
        in_specs=[SMEM, SMEM] + [VMEM] * 12,
        out_specs=[VMEM] * 2,
        scratch_shapes=[pltpu.VMEM((M + PCAP, LOADS), f32)],
        compiler_params=params(20),
        name="last",
    )(starts, lengths, modes, product, weight, residual, correction, multipliers, *received)


def coarse_kernel(slots, *rest):
    blocks, gathered, parts, scratch = rest[:8], rest[8:12], rest[12:20], rest[20]
    for group in range(4):
        for item in range(4):
            slot = slots[group * 4 + item]
            rows = pl.ds(pl.multiple_of(slot * NM, NM), NM)
            scratch[rows, :] = side_by_side(gathered[group][pl.ds(item * NM, NM), :])
    for block, part in zip(blocks, parts):
        high, low = split(block[...])
        both = dot(jnp.concatenate([high, low], axis=0), scratch[...])
        part[...] = fold(both[:NM] + both[NM:])


def coarse_product(slots, blocks, gathered):
    return pl.pallas_call(
        coarse_kernel,
        out_shape=[COEF] * 8,
        in_specs=[SMEM] + [VMEM] * 12,
        out_specs=[VMEM] * 8,
        scratch_shapes=[pltpu.VMEM((16 * NM, 2 * LOADS), bf16)],
        compiler_params=params(20),
        name="coarse",
    )(slots, *blocks, *gathered)


def project_kernel(starts, high, low, modes_t, multipliers, *rest):
    parts, outs, scratch = rest[:8], rest[8:16], rest[16:]
    new_multipliers, product = outs[:2]
    high_buf, low_buf, wide, padded, sems = scratch
    copies = start_operator(high, low, high_buf, low_buf, sems)
    amplitude = parts[0][...]
    for part in parts[1:]:
        amplitude = amplitude + part[...]
    amp_high, amp_low = split(amplitude)
    stacked = jnp.concatenate([amp_high, amp_high, amp_low], axis=0)
    moved = multipliers[...] - dot(modes_t[...], stacked)
    new_multipliers[...] = moved
    wide[...] = side_by_side(moved)
    apply_operator(copies, high_buf, low_buf, wide, padded)
    cut(starts, padded, product, outs[2:])


def project_step(starts, high, low, modes_t, multipliers, parts):
    return pl.pallas_call(
        project_kernel,
        out_shape=[VEC] * 2 + [PIECE] * 6,
        in_specs=[SMEM, ANY, ANY] + [VMEM] * 10,
        out_specs=[VMEM] * 8,
        scratch_shapes=OPERATOR_SCRATCH,
        compiler_params=params(32),
        name="project",
    )(starts, high, low, modes_t, multipliers, *parts)


def final_kernel(starts, lengths, product, weight, data, multipliers, *rest):
    received, (solution_out, residual_out, padded) = rest[:6], rest[6:]
    applied = place(starts, lengths, product, received, padded) * weight[...]
    residual_out[...] = (data[...] - applied).T
    solution_out[...] = multipliers[...].T


def final_step(starts, lengths, product, weight, data, multipliers, received):
    out = jax.ShapeDtypeStruct((LOADS, M), f32)
    return pl.pallas_call(
        final_kernel,
        out_shape=[out, out],
        in_specs=[SMEM, SMEM] + [VMEM] * 10,
        out_specs=[VMEM] * 2,
        scratch_shapes=[pltpu.VMEM((M + PCAP, LOADS), f32)],
        compiler_params=params(20),
        name="final",
    )(starts, lengths, product, weight, data, multipliers, *received)


def exchange(pieces):
    received = []
    for number, axes in enumerate((GX, GY, GZ)):
        count = lax.axis_size(axes)
        forward = [(i, (i + 1) % count) for i in range(count)]
        backward = [(target, source) for source, target in forward]
        received.append(lax.ppermute(pieces[2 * number + 1], axes, forward))
        received.append(lax.ppermute(pieces[2 * number], axes, backward))
    return received


def xor_pairs(count, mask):
    return [(i, i ^ mask) for i in range(count)]


def per_device(
    load_data,
    initial_dual,
    dual_operator,
    coarse_modes,
    coarse_inverse,
    face_start,
    face_len,
    multiplicity,
):
    starts = face_start[0, 0, 0]
    ends = []
    for axes in (GX, GY, GZ):
        ends += [lax.axis_index(axes) > 0, lax.axis_index(axes) < lax.axis_size(axes) - 1]
    lengths = jnp.where(jnp.stack(ends), face_len[0, 0, 0], 0)

    mine = lax.axis_index(RSG)
    blocks = []
    for mask in range(8):
        offset = (mine ^ mask) * 512
        block = jnp.concatenate(
            [
                lax.dynamic_slice(coarse_inverse, (0, half * 4096 + offset), (NM, 512))
                for half in range(2)
            ],
            axis=1,
        )
        blocks.append(block if mask == 0 else lax.ppermute(block, RSG, xor_pairs(8, mask)))

    along_x = lax.axis_index(("xh", "xl"))
    along_y = lax.axis_index("y")
    slots = []
    for y_mask in range(4):
        for x_mask in range(4):
            x = along_x ^ x_mask
            slots.append((x // 2) * 8 + (along_y ^ y_mask) * 2 + x % 2)
    slots = jnp.stack(slots).astype(jnp.int32)

    def gather(coeffs):
        line = [coeffs] + [
            lax.ppermute(coeffs, ("xh", "xl"), xor_pairs(4, mask)) for mask in range(1, 4)
        ]
        line = jnp.concatenate(line, axis=0)
        return [line] + [lax.ppermute(line, "y", xor_pairs(4, mask)) for mask in range(1, 4)]

    def scatter(parts):
        return [parts[0]] + [
            lax.ppermute(parts[mask], RSG, xor_pairs(8, mask)) for mask in range(1, 8)
        ]

    data, weight, modes_rows, modes_t = turn(
        load_data[0, 0, 0], multiplicity[0, 0], coarse_modes[0, 0, 0]
    )
    high, low, multipliers, product, *pieces = first_apply(
        starts, dual_operator[0, 0, 0], initial_dual[0, 0, 0]
    )
    received = exchange(pieces)
    for _ in range(OUTER):
        stretch = center / half_width
        rho = 1.0 / stretch
        residual, correction, multipliers, product, *pieces = start_step(
            starts, lengths, high, low, product, weight, data, multipliers, received
        )
        received = exchange(pieces)
        for index in range(1, CHEB):
            rho_next = 1.0 / (2.0 * stretch - rho)
            scale, gain = rho_next * rho, 2.0 * rho_next / half_width
            rho = rho_next
            if index < CHEB - 1:
                residual, correction, multipliers, product, *pieces = inner_step(
                    scale, gain, starts, lengths, high, low, product, weight,
                    residual, correction, multipliers, received,
                )
                received = exchange(pieces)
            else:
                multipliers, coeffs = last_step(
                    scale, gain, starts, lengths, modes_rows, product, weight,
                    residual, correction, multipliers, received,
                )
        parts = scatter(coarse_product(slots, blocks, gather(coeffs)))
        multipliers, product, *pieces = project_step(
            starts, high, low, modes_t, multipliers, parts
        )
        received = exchange(pieces)
    solved, final_residual = final_step(
        starts, lengths, product, weight, data, multipliers, received
    )
    return solved.reshape(initial_dual.shape), final_residual.reshape(initial_dual.shape)


def solution(mesh):
    fine = Mesh(mesh.devices.reshape(2, 2, 4, 4, 2), ("xh", "co", "gy", "y", "xl"))
    grid = (GX, "gy", GZ)
    placed = (
        P(*grid, None, None),
        P(*grid, None, None),
        P(*grid, None, None),
        P(*grid, None, None),
        P(("xh", "co", "gy", "y", "xl"), None),
        P(*grid, None),
        P(*grid, None),
        P(*grid, None),
    )
    return jax.shard_map(
        per_device,
        mesh=fine,
        in_specs=placed,
        out_specs=(P(*grid, None, None), P(*grid, None, None)),
        check_vma=False,
    )
```

```python
import functools

import jax
import jax.numpy as jnp
from jax import lax
from jax.experimental import pallas as pl
from jax.experimental.pallas import tpu as pltpu
from jax.sharding import Mesh, PartitionSpec as P

M = 1536
PCAP = 256
NM = 64
LOADS = 128
OUTER = 2
CHEB = 3
CHUNK = 256
NCHUNK = M // CHUNK


center = 1.0
half_width = 0.9

f32 = jnp.float32
bf16 = jnp.bfloat16

GX = ("xh", "co")
GY = ("gy",)
GZ = ("y", "xl")
RSG = ("co", "gy")

VEC = jax.ShapeDtypeStruct((M, LOADS), f32)
PIECE = jax.ShapeDtypeStruct((PCAP, LOADS), f32)
COEF = jax.ShapeDtypeStruct((NM, LOADS), f32)
VMEM = pl.BlockSpec(memory_space=pltpu.VMEM)
SMEM = pl.BlockSpec(memory_space=pltpu.SMEM)
HBM = pl.BlockSpec(memory_space=pltpu.HBM)

SLOTS = ((2, 1), (0, 1), (1, 1), (2, 0), (1, 0), (0, 0))


def split(x):
    high = x.astype(bf16)
    return high, (x - high.astype(f32)).astype(bf16)


def side_by_side(x):
    return jnp.concatenate(split(x), axis=1)


def fold(x):
    return x[:, :LOADS] + x[:, LOADS:]


def dot(a, b):
    return lax.dot_general(a, b, (((1,), (0,)), ((), ())), preferred_element_type=f32)


def apply_operator(high, low, wide, padded):
    for k in range(NCHUNK):
        rows = pl.ds(k * CHUNK, CHUNK)
        padded[rows, :] = fold(dot(high[rows, :], wide[...]) + dot(low[rows, :], wide[...]))
    padded[pl.ds(M, PCAP), :] = jnp.zeros((PCAP, LOADS), f32)


def cut(scalars, padded, product, pieces):
    product[...] = padded[pl.ds(0, M), :]
    for face in range(6):
        pieces[face][...] = padded[pl.ds(scalars[face], PCAP), :]


def place(scalars, product, received, padded):
    padded[pl.ds(0, M), :] = product[...]
    row = lax.broadcasted_iota(jnp.int32, (PCAP, LOADS), 0)
    for face in range(6):
        window = pl.ds(scalars[face], PCAP)
        padded[window, :] = padded[window, :] + jnp.where(
            row < scalars[6 + face], received[face][...], 0.0
        )
    return padded[pl.ds(0, M), :]


OPERATOR_SCRATCH = [
    pltpu.VMEM((M, 2 * LOADS), bf16),
    pltpu.VMEM((M + PCAP, LOADS), f32),
]


def params(megabytes):
    return pltpu.CompilerParams(vmem_limit_bytes=megabytes << 20)


def axis_position(axes):
    position = 0
    for name in axes:
        position = position * lax.axis_size(name) + lax.axis_index(name)
    return position


def first_kernel(
    start_in, len_in, operator, inverse, vectors, data, weight_in, modes, *rest
):
    outs, scratch = rest[:23], rest[23:]
    buffer, vector_buf, data_buf, modes_buf, weight_buf = scratch[:5]
    face_start, face_len, wide, padded, sems, block_sems = scratch[5:]
    high, low, vectors_t, product = outs[:4]
    pieces, blocks = outs[4:10], outs[10:18]
    data_t, weight_t, modes_rows, modes_t, scalars = outs[18:]
    small = []
    for source, target in ((start_in, face_start), (len_in, face_len), (weight_in, weight_buf)):
        copy = pltpu.make_async_copy(source, target, sems.at[NCHUNK + 3 + len(small)])
        copy.start()
        small.append(copy)
    fetch_vectors = pltpu.make_async_copy(vectors, vector_buf, sems.at[NCHUNK])
    fetch_vectors.start()
    copies = []
    for k in range(NCHUNK):
        rows = pl.ds(k * CHUNK, CHUNK)
        copy = pltpu.make_async_copy(operator.at[rows], buffer.at[rows], sems.at[k])
        copy.start()
        copies.append(copy)
    fetch_data = pltpu.make_async_copy(data, data_buf, sems.at[NCHUNK + 1])
    fetch_data.start()
    fetch_modes = pltpu.make_async_copy(modes, modes_buf, sems.at[NCHUNK + 2])
    fetch_modes.start()
    group = axis_position(RSG)
    moves = []
    for mask in range(8):
        for half in range(2):
            offset = pl.multiple_of((group ^ mask) * 512 + half * 4096, 512)
            move = pltpu.make_async_copy(
                inverse.at[:, pl.ds(offset, 512)],
                blocks[mask].at[:, pl.ds(half * 512, 512)],
                block_sems.at[mask, half],
            )
            move.start()
            moves.append(move)

    for copy in small:
        copy.wait()
    for slot, (number, kind) in enumerate(SLOTS):
        axes = (GX, GY, GZ)[number]
        position = axis_position(axes)
        count = lax.axis_size(axes)
        parity = position & 1
        face = 2 * number + (parity if kind else 1 - parity)
        length = face_len[face]
        if kind:
            length = jnp.where((position > 0) & (position < count - 1), length, 0)
        scalars[slot] = face_start[face]
        scalars[6 + slot] = length
    along_x = axis_position(("xh", "xl"))
    along_y = axis_position(("y",))
    for y_mask in range(4):
        for x_mask in range(4):
            x = along_x ^ x_mask
            scalars[12 + y_mask * 4 + x_mask] = (
                (x >> 1) * 8 + (along_y ^ y_mask) * 2 + (x & 1)
            )

    weight_t[...] = jnp.broadcast_to(1.0 / weight_buf[...].astype(f32), (LOADS, M)).T
    fetch_vectors.wait()
    turned = vector_buf[...].T
    vectors_t[...] = turned
    wide[...] = side_by_side(turned)
    for k in range(NCHUNK):
        copies[k].wait()
        rows = pl.ds(k * CHUNK, CHUNK)
        block_high, block_low = split(buffer[rows, :])
        high[rows, :] = block_high
        low[rows, :] = block_low
        padded[rows, :] = fold(dot(block_high, wide[...]) + dot(block_low, wide[...]))
    padded[pl.ds(M, PCAP), :] = jnp.zeros((PCAP, LOADS), f32)
    cut(scalars, padded, product, pieces)
    fetch_data.wait()
    data_t[...] = data_buf[...].T
    fetch_modes.wait()
    modes_high, modes_low = split(modes_buf[...])
    modes_rows[...] = jnp.concatenate([modes_high, modes_low], axis=0)
    modes_high, modes_low = split(modes_buf[...].T)
    modes_t[...] = jnp.concatenate([modes_high, modes_low, modes_high], axis=1)
    for move in moves:
        move.wait()


def first_apply(face_start, face_len, operator, inverse, vectors, data, multiplicity, modes):
    half = jax.ShapeDtypeStruct((M, M), bf16)
    block = jax.ShapeDtypeStruct((NM, 1024), f32)
    return pl.pallas_call(
        first_kernel,
        out_shape=[half, half, VEC, VEC]
        + [PIECE] * 6
        + [block] * 8
        + [
            VEC,
            VEC,
            jax.ShapeDtypeStruct((2 * NM, M), bf16),
            jax.ShapeDtypeStruct((M, 3 * NM), bf16),
            jax.ShapeDtypeStruct((28,), jnp.int32),
        ],
        in_specs=[HBM] * 8,
        out_specs=[VMEM] * 10 + [HBM] * 8 + [VMEM] * 4 + [SMEM],
        scratch_shapes=[
            pltpu.VMEM((M, M), f32),
            pltpu.VMEM((LOADS, M), f32),
            pltpu.VMEM((LOADS, M), f32),
            pltpu.VMEM((NM, M), f32),
            pltpu.VMEM((1, M), jnp.int32),
            pltpu.SMEM((6,), jnp.int32),
            pltpu.SMEM((6,), jnp.int32),
            pltpu.VMEM((M, 2 * LOADS), bf16),
            pltpu.VMEM((M + PCAP, LOADS), f32),
            pltpu.SemaphoreType.DMA((NCHUNK + 6,)),
            pltpu.SemaphoreType.DMA((8, 2)),
        ],
        compiler_params=params(24),
        name="first",
    )(
        *(
            pltpu.with_memory_space_constraint(array, pltpu.HBM)
            for array in (
                face_start, face_len, operator, inverse, vectors, data, multiplicity, modes
            )
        )
    )


def start_kernel(scalars, high, low, product, weight, data, multipliers, *rest):
    received, outs, scratch = rest[:6], rest[6:16], rest[16:]
    residual, correction, new_multipliers, new_product = outs[:4]
    wide, padded = scratch
    applied = place(scalars, product, received, padded) * weight[...]
    new_residual = data[...] - applied
    residual[...] = new_residual
    new_correction = new_residual / center
    correction[...] = new_correction
    new_multipliers[...] = multipliers[...] + new_correction
    wide[...] = side_by_side(new_correction)
    apply_operator(high, low, wide, padded)
    cut(scalars, padded, new_product, outs[4:])


def start_step(scalars, high, low, product, weight, data, multipliers, received):
    return pl.pallas_call(
        start_kernel,
        out_shape=[VEC] * 4 + [PIECE] * 6,
        in_specs=[SMEM] + [VMEM] * 12,
        out_specs=[VMEM] * 10,
        scratch_shapes=OPERATOR_SCRATCH,
        compiler_params=params(8),
        name="start",
    )(scalars, high, low, product, weight, data, multipliers, *received)


def inner_kernel(
    scale, gain, scalars, high, low, product, weight, residual, correction, multipliers, *rest
):
    received, outs, scratch = rest[:6], rest[6:16], rest[16:]
    new_residual, new_correction, new_multipliers, new_product = outs[:4]
    wide, padded = scratch
    applied = place(scalars, product, received, padded) * weight[...]
    remaining = residual[...] - applied
    new_residual[...] = remaining
    step = scale * correction[...] + gain * remaining
    new_correction[...] = step
    new_multipliers[...] = multipliers[...] + step
    wide[...] = side_by_side(step)
    apply_operator(high, low, wide, padded)
    cut(scalars, padded, new_product, outs[4:])


def inner_step(
    scale, gain, scalars, high, low, product, weight, residual, correction, multipliers, received
):
    return pl.pallas_call(
        functools.partial(inner_kernel, scale, gain),
        out_shape=[VEC] * 4 + [PIECE] * 6,
        in_specs=[SMEM] + [VMEM] * 13,
        out_specs=[VMEM] * 10,
        scratch_shapes=OPERATOR_SCRATCH,
        compiler_params=params(8),
        name="inner",
    )(scalars, high, low, product, weight, residual, correction, multipliers, *received)


def last_kernel(
    scale, gain, scalars, modes, product, weight, residual, correction, multipliers, *rest
):
    received, (new_multipliers, coeffs, padded) = rest[:6], rest[6:]
    applied = place(scalars, product, received, padded) * weight[...]
    remaining = residual[...] - applied
    step = scale * correction[...] + gain * remaining
    moved = multipliers[...] + step
    new_multipliers[...] = moved
    both = dot(modes[...], side_by_side(moved))
    coeffs[...] = fold(both[:NM] + both[NM:])


def last_step(
    scale, gain, scalars, modes, product, weight, residual, correction, multipliers, received
):
    return pl.pallas_call(
        functools.partial(last_kernel, scale, gain),
        out_shape=[VEC, COEF],
        in_specs=[SMEM] + [VMEM] * 12,
        out_specs=[VMEM] * 2,
        scratch_shapes=[pltpu.VMEM((M + PCAP, LOADS), f32)],
        compiler_params=params(8),
        name="last",
    )(scalars, modes, product, weight, residual, correction, multipliers, *received)


def join_kernel(*refs):
    out = refs[-1]
    for k, ref in enumerate(refs[:-1]):
        out[pl.ds(k * NM, NM), :] = ref[...]


def join(pieces):
    return pl.pallas_call(
        join_kernel,
        out_shape=jax.ShapeDtypeStruct((len(pieces) * NM, LOADS), f32),
        in_specs=[VMEM] * len(pieces),
        out_specs=VMEM,
        compiler_params=params(4),
        name="join",
    )(*pieces)


def blocks_kernel(*refs):
    out = refs[-1]
    for mask, block in enumerate(refs[:-1]):
        high, low = split(block[...])
        out[pl.ds(mask * NM, NM), :] = high
        out[pl.ds((8 + mask) * NM, NM), :] = low


def prepare_blocks(blocks):
    return pl.pallas_call(
        blocks_kernel,
        out_shape=jax.ShapeDtypeStruct((16 * NM, 16 * NM), bf16),
        in_specs=[VMEM] * 8,
        out_specs=VMEM,
        compiler_params=params(8),
        name="blocks",
    )(*blocks)


def coarse_kernel(scalars, blocks, *rest):
    gathered, parts, scratch = rest[:4], rest[4:8], rest[8]
    for group in range(4):
        for item in range(4):
            slot = scalars[12 + group * 4 + item]
            rows = pl.ds(pl.multiple_of(slot * NM, NM), NM)
            scratch[rows, :] = side_by_side(gathered[group][pl.ds(item * NM, NM), :])
    half = 8 * NM
    both = dot(blocks[pl.ds(0, half), :], scratch[...])
    both = fold(both + dot(blocks[pl.ds(half, half), :], scratch[...]))
    for mask in range(8):
        parts[mask % 4][pl.ds(mask // 4 * NM, NM), :] = both[mask * NM : (mask + 1) * NM]


def coarse_product(scalars, blocks, gathered):
    return pl.pallas_call(
        coarse_kernel,
        out_shape=[jax.ShapeDtypeStruct((2 * NM, LOADS), f32)] * 4,
        in_specs=[SMEM] + [VMEM] * 5,
        out_specs=[VMEM] * 4,
        scratch_shapes=[pltpu.VMEM((16 * NM, 2 * LOADS), bf16)],
        compiler_params=params(8),
        name="coarse",
    )(scalars, blocks, *gathered)


def sum_kernel(*refs):
    parts, (kept, sent) = refs[:4], refs[4:]
    kept[...] = sum(part[pl.ds(0, NM), :] for part in parts[1:]) + parts[0][pl.ds(0, NM), :]
    sent[...] = sum(part[pl.ds(NM, NM), :] for part in parts[1:]) + parts[0][pl.ds(NM, NM), :]


def sum_parts(parts):
    return pl.pallas_call(
        sum_kernel,
        out_shape=[COEF] * 2,
        in_specs=[VMEM] * 4,
        out_specs=[VMEM] * 2,
        compiler_params=params(4),
        name="sum",
    )(*parts)


def project_kernel(scalars, high, low, modes_t, multipliers, kept, partner, *rest):
    (new_multipliers, product), pieces, (wide, padded) = rest[:2], rest[2:8], rest[8:]
    amp_high, amp_low = split(kept[...] + partner[...])
    stacked = jnp.concatenate([amp_high, amp_high, amp_low], axis=0)
    moved = multipliers[...] - dot(modes_t[...], stacked)
    new_multipliers[...] = moved
    wide[...] = side_by_side(moved)
    apply_operator(high, low, wide, padded)
    cut(scalars, padded, product, pieces)


def project_step(scalars, high, low, modes_t, multipliers, kept, partner):
    return pl.pallas_call(
        project_kernel,
        out_shape=[VEC] * 2 + [PIECE] * 6,
        in_specs=[SMEM] + [VMEM] * 6,
        out_specs=[VMEM] * 8,
        scratch_shapes=OPERATOR_SCRATCH,
        compiler_params=params(8),
        name="project",
    )(scalars, high, low, modes_t, multipliers, kept, partner)


def final_kernel(scalars, product, weight, data, multipliers, *rest):
    received, (solution_out, residual_out, padded) = rest[:6], rest[6:]
    applied = place(scalars, product, received, padded) * weight[...]
    residual_out[...] = (data[...] - applied).T
    solution_out[...] = multipliers[...].T


def final_step(scalars, product, weight, data, multipliers, received):
    out = jax.ShapeDtypeStruct((LOADS, M), f32)
    return pl.pallas_call(
        final_kernel,
        out_shape=[out, out],
        in_specs=[SMEM] + [VMEM] * 10,
        out_specs=[VMEM] * 2,
        scratch_shapes=[pltpu.VMEM((M + PCAP, LOADS), f32)],
        compiler_params=params(8),
        name="final",
    )(scalars, product, weight, data, multipliers, *received)


def swap_pairs(count, odd):
    lower = range(odd, count, 2)
    pairs = [(i, (i + 1) % count) for i in lower]
    return pairs + [(target, source) for source, target in pairs]


def exchange(pieces):
    received = []
    for piece, (number, kind) in zip(pieces, SLOTS):
        axes = (GX, GY, GZ)[number]
        received.append(lax.ppermute(piece, axes, swap_pairs(lax.axis_size(axes), kind)))
    return received


def xor_pairs(count, mask):
    return [(i, i ^ mask) for i in range(count)]


def per_device(
    load_data,
    initial_dual,
    dual_operator,
    coarse_modes,
    coarse_inverse,
    face_start,
    face_len,
    multiplicity,
):
    def gather(coeffs):
        line = join(
            [coeffs]
            + [lax.ppermute(coeffs, ("xh", "xl"), xor_pairs(4, mask)) for mask in range(1, 4)]
        )
        return [line] + [lax.ppermute(line, "y", xor_pairs(4, mask)) for mask in range(1, 4)]

    def scatter(parts):
        kept, sent = sum_parts(
            [parts[0]]
            + [lax.ppermute(parts[mask], "gy", xor_pairs(4, mask)) for mask in range(1, 4)]
        )
        return kept, lax.ppermute(sent, "co", xor_pairs(2, 1))

    high, low, multipliers, product, *rest = first_apply(
        face_start[0, 0, 0],
        face_len[0, 0, 0],
        dual_operator[0, 0, 0],
        coarse_inverse,
        initial_dual[0, 0, 0],
        load_data[0, 0, 0],
        multiplicity[0, 0],
        coarse_modes[0, 0, 0],
    )
    pieces, blocks, (data, weight, modes_rows, modes_t, scalars) = rest[:6], rest[6:14], rest[14:]
    blocks = prepare_blocks(
        [
            block if mask == 0 else lax.ppermute(block, RSG, xor_pairs(8, mask))
            for mask, block in enumerate(blocks)
        ]
    )
    received = exchange(pieces)
    for _ in range(OUTER):
        stretch = center / half_width
        rho = 1.0 / stretch
        residual, correction, multipliers, product, *pieces = start_step(
            scalars, high, low, product, weight, data, multipliers, received
        )
        received = exchange(pieces)
        for index in range(1, CHEB):
            rho_next = 1.0 / (2.0 * stretch - rho)
            scale, gain = rho_next * rho, 2.0 * rho_next / half_width
            rho = rho_next
            if index < CHEB - 1:
                residual, correction, multipliers, product, *pieces = inner_step(
                    scale, gain, scalars, high, low, product, weight,
                    residual, correction, multipliers, received,
                )
                received = exchange(pieces)
            else:
                multipliers, coeffs = last_step(
                    scale, gain, scalars, modes_rows, product, weight,
                    residual, correction, multipliers, received,
                )
        kept, partner = scatter(coarse_product(scalars, blocks, gather(coeffs)))
        multipliers, product, *pieces = project_step(
            scalars, high, low, modes_t, multipliers, kept, partner
        )
        received = exchange(pieces)
    solved, final_residual = final_step(
        scalars, product, weight, data, multipliers, received
    )
    return solved.reshape(initial_dual.shape), final_residual.reshape(initial_dual.shape)


def solution(mesh):
    fine = Mesh(mesh.devices.reshape(2, 2, 4, 4, 2), ("xh", "co", "gy", "y", "xl"))
    grid = (GX, "gy", GZ)
    placed = (
        P(*grid, None, None),
        P(*grid, None, None),
        P(*grid, None, None),
        P(*grid, None, None),
        P(("xh", "co", "gy", "y", "xl"), None),
        P(*grid, None),
        P(*grid, None),
        P(*grid, None),
    )
    return jax.shard_map(
        per_device,
        mesh=fine,
        in_specs=placed,
        out_specs=(P(*grid, None, None), P(*grid, None, None)),
        check_vma=False,
    )
```

```python
import functools

import jax
import jax.numpy as jnp
from jax import lax
from jax.experimental import pallas as pl
from jax.experimental.pallas import tpu as pltpu
from jax.sharding import Mesh, PartitionSpec as P

M = 1536
PCAP = 256
NM = 64
LOADS = 128
OUTER = 2
CHEB = 3
CHUNK = 256
NCHUNK = M // CHUNK
STRIP = 384


center = 1.0
half_width = 0.9

f32 = jnp.float32
bf16 = jnp.bfloat16

GX = ("xh", "co")
GY = ("gy",)
GZ = ("y", "xl")
RSG = ("co", "gy")


def recurrence():
    stretch = center / half_width
    rho = 1.0 / stretch
    gains = []
    for _ in range(CHEB - 1):
        rho_next = 1.0 / (2.0 * stretch - rho)
        gains.append((rho_next * rho, 2.0 * rho_next / half_width))
        rho = rho_next
    return gains


GAINS = recurrence()

VEC = jax.ShapeDtypeStruct((M, LOADS), f32)
PADDED = jax.ShapeDtypeStruct((M + PCAP, LOADS), f32)
PIECE = jax.ShapeDtypeStruct((PCAP, LOADS), f32)
PAIR = jax.ShapeDtypeStruct((2,), f32)
COEF = jax.ShapeDtypeStruct((NM, LOADS), f32)
VMEM = pl.BlockSpec(memory_space=pltpu.VMEM)
SMEM = pl.BlockSpec(memory_space=pltpu.SMEM)
HBM = pl.BlockSpec(memory_space=pltpu.HBM)

WINDOWS = ((), (2, 4, 5), (6, 7))

SLOTS = ((2, 1), (0, 1), (1, 1), (2, 0), (1, 0), (0, 0))


def split(x):
    high = x.astype(bf16)
    return high, (x - high.astype(f32)).astype(bf16)


def side_by_side(x):
    return jnp.concatenate(split(x), axis=1)


def fold(x):
    return x[:, :LOADS] + x[:, LOADS:]


def dot(a, b):
    return lax.dot_general(a, b, (((1,), (0,)), ((), ())), preferred_element_type=f32)


def apply_operator(high, low, wide, padded):
    for k in range(NCHUNK):
        rows = pl.ds(k * CHUNK, CHUNK)
        padded[rows, :] = fold(dot(high[rows, :], wide[...]) + dot(low[rows, :], wide[...]))
    padded[pl.ds(M, PCAP), :] = jnp.zeros((PCAP, LOADS), f32)


def cut(scalars, padded, pieces):
    for face in range(6):
        pieces[face][...] = padded[pl.ds(scalars[face], PCAP), :]


def place(scalars, product, received, padded):
    padded[pl.ds(0, M), :] = product[pl.ds(0, M), :]
    row = lax.broadcasted_iota(jnp.int32, (PCAP, LOADS), 0)
    for face in range(6):
        window = pl.ds(scalars[face], PCAP)
        padded[window, :] = padded[window, :] + jnp.where(
            row < scalars[6 + face], received[face][...], 0.0
        )
    return padded[pl.ds(0, M), :]


OPERATOR_SCRATCH = [
    pltpu.VMEM((M, 2 * LOADS), bf16),
    pltpu.VMEM((M + PCAP, LOADS), f32),
]


def params(megabytes):
    return pltpu.CompilerParams(vmem_limit_bytes=megabytes << 20)


def axis_position(axes):
    position = 0
    for name in axes:
        position = position * lax.axis_size(name) + lax.axis_index(name)
    return position


def first_kernel(start_in, len_in, operator, vectors, *rest):
    (high, low, vectors_t, product), pieces, scratch = rest[:4], rest[4:10], rest[12:]
    scalars, gains = rest[10:12]
    gains[0], gains[1] = 0.0, 1.0 / center
    buffer, vector_buf, face_start, face_len, wide, sems = scratch

    def chunk_copy(k):
        rows = pl.ds(pl.multiple_of(k * CHUNK, CHUNK), CHUNK)
        return pltpu.make_async_copy(operator.at[rows], buffer.at[rows], sems.at[k])

    small = []
    for source, target in ((start_in, face_start), (len_in, face_len), (vectors, vector_buf)):
        copy = pltpu.make_async_copy(source, target, sems.at[NCHUNK + len(small)])
        copy.start()
        small.append(copy)
    for k in range(NCHUNK):
        chunk_copy(k).start()
    small[0].wait()
    small[1].wait()
    for slot, (number, kind) in enumerate(SLOTS):
        axes = (GX, GY, GZ)[number]
        position = axis_position(axes)
        count = lax.axis_size(axes)
        parity = position & 1
        face = 2 * number + (parity if kind else 1 - parity)
        length = face_len[face]
        if kind:
            length = jnp.where((position > 0) & (position < count - 1), length, 0)
        scalars[slot] = face_start[face]
        scalars[6 + slot] = length
    along_x = axis_position(("xh", "xl"))
    along_y = axis_position(("y",))
    for y_mask in range(4):
        for x_mask in range(4):
            x = along_x ^ x_mask
            scalars[12 + y_mask * 4 + x_mask] = (
                (x >> 1) * 8 + (along_y ^ y_mask) * 2 + (x & 1)
            )
    group = axis_position(RSG)
    for mask in range(8):
        scalars[28 + mask] = (group ^ mask) * 512
    small[2].wait()
    turned = vector_buf[...].T
    vectors_t[...] = turned
    wide[...] = side_by_side(turned)
    product[pl.ds(M, PCAP), :] = jnp.zeros((PCAP, LOADS), f32)

    def chunk(k, carry):
        chunk_copy(k).wait()
        rows = pl.ds(pl.multiple_of(k * CHUNK, CHUNK), CHUNK)
        block_high, block_low = split(buffer[rows, :])
        high[rows, :] = block_high
        low[rows, :] = block_low
        product[rows, :] = fold(dot(block_high, wide[...]) + dot(block_low, wide[...]))
        return carry

    lax.fori_loop(0, NCHUNK, chunk, 0)
    cut(scalars, product, pieces)


def in_hbm(*arrays):
    return [pltpu.with_memory_space_constraint(array, pltpu.HBM) for array in arrays]


def first_apply(face_start, face_len, operator, vectors):
    half = jax.ShapeDtypeStruct((M, M), bf16)
    return pl.pallas_call(
        first_kernel,
        out_shape=[half, half, VEC, PADDED]
        + [PIECE] * 6
        + [jax.ShapeDtypeStruct((36,), jnp.int32), PAIR],
        in_specs=[HBM] * 4,
        out_specs=[VMEM] * 10 + [SMEM] * 2,
        scratch_shapes=[
            pltpu.VMEM((M, M), f32),
            pltpu.VMEM((LOADS, M), f32),
            pltpu.SMEM((6,), jnp.int32),
            pltpu.SMEM((6,), jnp.int32),
            pltpu.VMEM((M, 2 * LOADS), bf16),
            pltpu.SemaphoreType.DMA((NCHUNK + 3,)),
        ],
        compiler_params=params(20),
        name="first",
    )(*in_hbm(face_start, face_len, operator, vectors))


def turn_kernel(scalars, data, weight, modes, inverse, *rest):
    (data_t, weight_t, modes_rows, modes_t), blocks, scratch = rest[:4], rest[4:12], rest[12:]
    data_buf, weight_buf, modes_buf, inverse_buf, sems = scratch
    copies = []
    for source, target in (
        (weight, weight_buf), (modes, modes_buf), (data, data_buf), (inverse, inverse_buf)
    ):
        copy = pltpu.make_async_copy(source, target, sems.at[len(copies)])
        copy.start()
        copies.append(copy)
    for copy in copies[:3]:
        copy.wait()

    def strip(k, carry):
        span = pl.ds(pl.multiple_of(k * STRIP, STRIP), STRIP)
        data_t[span, :] = data_buf[:, span].T
        weights = 1.0 / weight_buf[:, span].astype(f32)
        weight_t[span, :] = jnp.broadcast_to(weights, (LOADS, STRIP)).T
        high, low = split(modes_buf[:, span])
        modes_rows[:, span] = jnp.concatenate([high, low], axis=0)
        high, low = split(modes_buf[:, span].T)
        modes_t[span, :] = jnp.concatenate([high, low, high], axis=1)
        return carry

    lax.fori_loop(0, M // STRIP, strip, 0)
    copies[3].wait()
    for mask in range(8):
        for half in range(2):
            offset = pl.multiple_of(scalars[28 + mask] + half * 4096, 512)
            blocks[mask][:, pl.ds(half * 512, 512)] = inverse_buf[:, pl.ds(offset, 512)]


def turn(scalars, data, weight, modes, inverse):
    return pl.pallas_call(
        turn_kernel,
        out_shape=[
            VEC,
            VEC,
            jax.ShapeDtypeStruct((2 * NM, M), bf16),
            jax.ShapeDtypeStruct((M, 3 * NM), bf16),
        ]
        + [jax.ShapeDtypeStruct((NM, 1024), f32)] * 8,
        in_specs=[SMEM] + [HBM] * 4,
        out_specs=[VMEM] * 12,
        scratch_shapes=[
            pltpu.VMEM((LOADS, M), f32),
            pltpu.VMEM((1, M), jnp.int32),
            pltpu.VMEM((NM, M), f32),
            pltpu.VMEM((NM, 8192), f32),
            pltpu.SemaphoreType.DMA((4,)),
        ],
        compiler_params=params(8),
        name="turn",
    )(scalars, *in_hbm(data, weight, modes, inverse))


def step_kernel(
    scalars, gains, high, low, product, weight, residual, correction, multipliers, *rest
):
    received, outs, scratch = rest[:6], rest[6:17], rest[17:]
    new_residual, new_correction, new_multipliers, new_product = outs[:4]
    new_gains = outs[10]
    wide, padded = scratch
    applied = place(scalars, product, received, padded) * weight[...]
    remaining = residual[...] - applied
    new_residual[...] = remaining
    step = gains[0] * correction[...] + gains[1] * remaining
    new_correction[...] = step
    new_multipliers[...] = multipliers[...] + step
    wide[...] = side_by_side(step)
    apply_operator(high, low, wide, new_product)
    cut(scalars, new_product, outs[4:10])
    new_gains[0], new_gains[1] = GAINS[0]


def step(scalars, gains, high, low, product, weight, residual, correction, multipliers, received):
    return pl.pallas_call(
        step_kernel,
        out_shape=[VEC] * 3 + [PADDED] + [PIECE] * 6 + [PAIR],
        in_specs=[SMEM, SMEM] + [VMEM] * 13,
        out_specs=[VMEM] * 10 + [SMEM],
        scratch_shapes=OPERATOR_SCRATCH,
        compiler_params=params(8),
        name="step",
    )(
        scalars, gains, high, low, product, weight, residual, correction, multipliers, *received
    )


def last_kernel(
    scale, gain, scalars, modes, product, weight, residual, correction, multipliers, *rest
):
    received, (new_multipliers, coeffs, padded) = rest[:6], rest[6:]
    applied = place(scalars, product, received, padded) * weight[...]
    remaining = residual[...] - applied
    step = scale * correction[...] + gain * remaining
    moved = multipliers[...] + step
    new_multipliers[...] = moved
    both = dot(modes[...], side_by_side(moved))
    coeffs[...] = fold(both[:NM] + both[NM:])


def last_step(
    scale, gain, scalars, modes, product, weight, residual, correction, multipliers, received
):
    return pl.pallas_call(
        functools.partial(last_kernel, scale, gain),
        out_shape=[VEC, COEF],
        in_specs=[SMEM] + [VMEM] * 12,
        out_specs=[VMEM] * 2,
        scratch_shapes=[pltpu.VMEM((M + PCAP, LOADS), f32)],
        compiler_params=params(8),
        name="last",
    )(scalars, modes, product, weight, residual, correction, multipliers, *received)


def join_kernel(*refs):
    out = refs[-1]
    for k, ref in enumerate(refs[:-1]):
        out[pl.ds(k * NM, NM), :] = ref[...]


def join(pieces):
    return pl.pallas_call(
        join_kernel,
        out_shape=jax.ShapeDtypeStruct((len(pieces) * NM, LOADS), f32),
        in_specs=[VMEM] * len(pieces),
        out_specs=VMEM,
        compiler_params=params(4),
        name="join",
    )(*pieces)


def blocks_kernel(*refs):
    out = refs[-1]
    for mask, block in enumerate(refs[:-1]):
        high, low = split(block[...])
        out[pl.ds(mask * NM, NM), :] = high
        out[pl.ds((8 + mask) * NM, NM), :] = low


def prepare_blocks(blocks):
    return pl.pallas_call(
        blocks_kernel,
        out_shape=jax.ShapeDtypeStruct((16 * NM, 16 * NM), bf16),
        in_specs=[VMEM] * 8,
        out_specs=VMEM,
        compiler_params=params(8),
        name="blocks",
    )(*blocks)


def coarse_kernel(scalars, blocks, *rest):
    gathered, parts, scratch = rest[:4], rest[4:8], rest[8]
    for group in range(4):
        for item in range(4):
            slot = scalars[12 + group * 4 + item]
            rows = pl.ds(pl.multiple_of(slot * NM, NM), NM)
            scratch[rows, :] = side_by_side(gathered[group][pl.ds(item * NM, NM), :])
    half = 8 * NM
    both = dot(blocks[pl.ds(0, half), :], scratch[...])
    both = fold(both + dot(blocks[pl.ds(half, half), :], scratch[...]))
    for mask in range(8):
        parts[mask % 4][pl.ds(mask // 4 * NM, NM), :] = both[mask * NM : (mask + 1) * NM]


def coarse_product(scalars, blocks, gathered):
    return pl.pallas_call(
        coarse_kernel,
        out_shape=[jax.ShapeDtypeStruct((2 * NM, LOADS), f32)] * 4,
        in_specs=[SMEM] + [VMEM] * 5,
        out_specs=[VMEM] * 4,
        scratch_shapes=[pltpu.VMEM((16 * NM, 2 * LOADS), bf16)],
        compiler_params=params(8),
        name="coarse",
    )(scalars, blocks, *gathered)


def sum_kernel(*refs):
    parts, (kept, sent) = refs[:4], refs[4:]
    kept[...] = sum(part[pl.ds(0, NM), :] for part in parts[1:]) + parts[0][pl.ds(0, NM), :]
    sent[...] = sum(part[pl.ds(NM, NM), :] for part in parts[1:]) + parts[0][pl.ds(NM, NM), :]


def sum_parts(parts):
    return pl.pallas_call(
        sum_kernel,
        out_shape=[COEF] * 2,
        in_specs=[VMEM] * 4,
        out_specs=[VMEM] * 2,
        compiler_params=params(4),
        name="sum",
    )(*parts)


def project_kernel(scalars, high, low, modes_t, multipliers, kept, partner, *rest):
    (new_multipliers, product), pieces, (gains, wide) = rest[:2], rest[2:8], rest[8:]
    gains[0], gains[1] = 0.0, 1.0 / center
    amp_high, amp_low = split(kept[...] + partner[...])
    stacked = jnp.concatenate([amp_high, amp_high, amp_low], axis=0)
    moved = multipliers[...] - dot(modes_t[...], stacked)
    new_multipliers[...] = moved
    wide[...] = side_by_side(moved)
    apply_operator(high, low, wide, product)
    cut(scalars, product, pieces)


def project_step(scalars, high, low, modes_t, multipliers, kept, partner):
    return pl.pallas_call(
        project_kernel,
        out_shape=[VEC, PADDED] + [PIECE] * 6 + [PAIR],
        in_specs=[SMEM] + [VMEM] * 6,
        out_specs=[VMEM] * 8 + [SMEM],
        scratch_shapes=OPERATOR_SCRATCH[:1],
        compiler_params=params(8),
        name="project",
    )(scalars, high, low, modes_t, multipliers, kept, partner)


def final_kernel(scalars, product, weight, data, multipliers, *rest):
    received, (solution_out, residual_out, padded) = rest[:6], rest[6:]
    applied = place(scalars, product, received, padded) * weight[...]
    residual_out[...] = (data[...] - applied).T
    solution_out[...] = multipliers[...].T


def final_step(scalars, product, weight, data, multipliers, received):
    out = jax.ShapeDtypeStruct((LOADS, M), f32)
    return pl.pallas_call(
        final_kernel,
        out_shape=[out, out],
        in_specs=[SMEM] + [VMEM] * 10,
        out_specs=[VMEM] * 2,
        scratch_shapes=[pltpu.VMEM((M + PCAP, LOADS), f32)],
        compiler_params=params(8),
        name="final",
    )(scalars, product, weight, data, multipliers, *received)


def swap_pairs(count, odd):
    lower = range(odd, count, 2)
    pairs = [(i, (i + 1) % count) for i in lower]
    return pairs + [(target, source) for source, target in pairs]


def exchange(pieces):
    received = []
    for piece, (number, kind) in zip(pieces, SLOTS):
        axes = (GX, GY, GZ)[number]
        received.append(lax.ppermute(piece, axes, swap_pairs(lax.axis_size(axes), kind)))
    return received


def xor_pairs(count, mask):
    return [(i, i ^ mask) for i in range(count)]


def per_device(
    load_data,
    initial_dual,
    dual_operator,
    coarse_modes,
    coarse_inverse,
    face_start,
    face_len,
    multiplicity,
):
    def gather(coeffs):
        line = join(
            [coeffs]
            + [lax.ppermute(coeffs, ("xh", "xl"), xor_pairs(4, mask)) for mask in range(1, 4)]
        )
        return [line] + [lax.ppermute(line, "y", xor_pairs(4, mask)) for mask in range(1, 4)]

    def scatter(parts):
        kept, sent = sum_parts(
            [parts[0]]
            + [lax.ppermute(parts[mask], "gy", xor_pairs(4, mask)) for mask in range(1, 4)]
        )
        return kept, lax.ppermute(sent, "co", xor_pairs(2, 1))

    high, low, multipliers, product, *pieces, scalars, gains = first_apply(
        face_start[0, 0, 0], face_len[0, 0, 0], dual_operator[0, 0, 0], initial_dual[0, 0, 0]
    )
    data, weight, modes_rows, modes_t, *blocks = turn(
        scalars, load_data[0, 0, 0], multiplicity[0, 0], coarse_modes[0, 0, 0], coarse_inverse
    )

    def move_blocks(received, masks):
        for mask in masks:
            blocks[mask] = lax.ppermute(blocks[mask], RSG, xor_pairs(8, mask))
        moved = [blocks[mask] for mask in masks]
        received, moved = lax.optimization_barrier((received, moved))
        for mask, block in zip(masks, moved):
            blocks[mask] = block
        return received

    received = exchange(pieces)
    for outer in range(OUTER):
        residual = correction = data
        for index in range(CHEB - 1):
            if outer == 0:
                received = move_blocks(received, WINDOWS[index])
            residual, correction, multipliers, product, *pieces, gains = step(
                scalars, gains, high, low, product, weight,
                residual, correction, multipliers, received,
            )
            received = exchange(pieces)
        if outer == 0:
            received = move_blocks(received, WINDOWS[-1])
            for mask in (1, 3):
                blocks[mask] = lax.ppermute(blocks[mask], RSG, xor_pairs(8, mask))
            prepared = prepare_blocks(blocks)
        multipliers, coeffs = last_step(
            *GAINS[-1], scalars, modes_rows, product, weight,
            residual, correction, multipliers, received,
        )
        kept, partner = scatter(coarse_product(scalars, prepared, gather(coeffs)))
        multipliers, product, *pieces, gains = project_step(
            scalars, high, low, modes_t, multipliers, kept, partner
        )
        received = exchange(pieces)
    solved, final_residual = final_step(
        scalars, product, weight, data, multipliers, received
    )
    return solved.reshape(initial_dual.shape), final_residual.reshape(initial_dual.shape)


def solution(mesh):
    fine = Mesh(mesh.devices.reshape(2, 2, 4, 4, 2), ("xh", "co", "gy", "y", "xl"))
    grid = (GX, "gy", GZ)
    placed = (
        P(*grid, None, None),
        P(*grid, None, None),
        P(*grid, None, None),
        P(*grid, None, None),
        P(("xh", "co", "gy", "y", "xl"), None),
        P(*grid, None),
        P(*grid, None),
        P(*grid, None),
    )
    return jax.shard_map(
        per_device,
        mesh=fine,
        in_specs=placed,
        out_specs=(P(*grid, None, None), P(*grid, None, None)),
        check_vma=False,
    )
```

```python
import functools

import jax
import jax.numpy as jnp
from jax import lax
from jax.experimental import pallas as pl
from jax.experimental.pallas import tpu as pltpu
from jax.sharding import Mesh, PartitionSpec as P

M = 1536
PCAP = 256
NM = 64
LOADS = 128
OUTER = 2
CHEB = 3
CHUNK = 256
NCHUNK = M // CHUNK
STRIP = 768
WIDE_CHUNK = 512


center = 1.0
half_width = 0.9

f32 = jnp.float32
bf16 = jnp.bfloat16

GX = ("xh", "co")
GY = ("gy",)
GZ = ("y", "xl")
RSG = ("co", "gy")


def recurrence():
    stretch = center / half_width
    rho = 1.0 / stretch
    gains = []
    for _ in range(CHEB - 1):
        rho_next = 1.0 / (2.0 * stretch - rho)
        gains.append((rho_next * rho, 2.0 * rho_next / half_width))
        rho = rho_next
    return gains


GAINS = recurrence()

VEC = jax.ShapeDtypeStruct((M, LOADS), f32)
PADDED = jax.ShapeDtypeStruct((M + PCAP, LOADS), f32)
PIECE = jax.ShapeDtypeStruct((PCAP, LOADS), f32)
PAIR = jax.ShapeDtypeStruct((2,), f32)
COEF = jax.ShapeDtypeStruct((NM, LOADS), f32)
VMEM = pl.BlockSpec(memory_space=pltpu.VMEM)
SMEM = pl.BlockSpec(memory_space=pltpu.SMEM)
HBM = pl.BlockSpec(memory_space=pltpu.HBM)

WINDOWS = ((), (2, 4, 5), (6, 7))

SLOTS = ((2, 1), (0, 1), (1, 1), (2, 0), (1, 0), (0, 0))


def split(x):
    high = x.astype(bf16)
    return high, (x - high.astype(f32)).astype(bf16)


def side_by_side(x):
    return jnp.concatenate(split(x), axis=1)


def fold(x):
    return x[:, :LOADS] + x[:, LOADS:]


def dot(a, b):
    return lax.dot_general(a, b, (((1,), (0,)), ((), ())), preferred_element_type=f32)


def apply_operator(high, low, wide, padded):
    for k in range(NCHUNK):
        rows = pl.ds(k * CHUNK, CHUNK)
        padded[rows, :] = fold(dot(high[rows, :], wide[...]) + dot(low[rows, :], wide[...]))
    padded[pl.ds(M, PCAP), :] = jnp.zeros((PCAP, LOADS), f32)


def cut(scalars, padded, pieces):
    for face in range(6):
        pieces[face][...] = padded[pl.ds(scalars[face], PCAP), :]


def place(scalars, product, received, padded):
    padded[pl.ds(0, M), :] = product[pl.ds(0, M), :]
    row = lax.broadcasted_iota(jnp.int32, (PCAP, LOADS), 0)
    for face in range(6):
        window = pl.ds(scalars[face], PCAP)
        padded[window, :] = padded[window, :] + jnp.where(
            row < scalars[6 + face], received[face][...], 0.0
        )
    return padded[pl.ds(0, M), :]


OPERATOR_SCRATCH = [
    pltpu.VMEM((M, 2 * LOADS), bf16),
    pltpu.VMEM((M + PCAP, LOADS), f32),
]


def params(megabytes):
    return pltpu.CompilerParams(vmem_limit_bytes=megabytes << 20)


def axis_position(axes):
    position = 0
    for name in axes:
        position = position * lax.axis_size(name) + lax.axis_index(name)
    return position


def first_kernel(start_in, len_in, operator, vectors, *rest):
    (high, low, vectors_t, product), pieces, scratch = rest[:4], rest[4:10], rest[12:]
    scalars, gains = rest[10:12]
    gains[0], gains[1] = 0.0, 1.0 / center
    buffer, vector_buf, face_start, face_len, wide, sems = scratch

    def chunk_copy(k):
        rows = pl.ds(pl.multiple_of(k * CHUNK, CHUNK), CHUNK)
        return pltpu.make_async_copy(operator.at[rows], buffer.at[rows], sems.at[k])

    small = []
    for source, target in ((start_in, face_start), (len_in, face_len), (vectors, vector_buf)):
        copy = pltpu.make_async_copy(source, target, sems.at[NCHUNK + len(small)])
        copy.start()
        small.append(copy)
    for k in range(NCHUNK):
        chunk_copy(k).start()
    small[0].wait()
    small[1].wait()
    for slot, (number, kind) in enumerate(SLOTS):
        axes = (GX, GY, GZ)[number]
        position = axis_position(axes)
        count = lax.axis_size(axes)
        parity = position & 1
        face = 2 * number + (parity if kind else 1 - parity)
        length = face_len[face]
        if kind:
            length = jnp.where((position > 0) & (position < count - 1), length, 0)
        scalars[slot] = face_start[face]
        scalars[6 + slot] = length
    along_x = axis_position(("xh", "xl"))
    along_y = axis_position(("y",))
    for y_mask in range(4):
        for x_mask in range(4):
            x = along_x ^ x_mask
            scalars[12 + y_mask * 4 + x_mask] = (
                (x >> 1) * 8 + (along_y ^ y_mask) * 2 + (x & 1)
            )
    group = axis_position(RSG)
    for mask in range(8):
        scalars[28 + mask] = (group ^ mask) * 512
    small[2].wait()
    turned = vector_buf[...].T
    vectors_t[...] = turned
    wide[...] = side_by_side(turned)
    product[pl.ds(M, PCAP), :] = jnp.zeros((PCAP, LOADS), f32)

    def chunk(k, carry):
        chunk_copy(k).wait()
        rows = pl.ds(pl.multiple_of(k * CHUNK, CHUNK), CHUNK)
        block_high, block_low = split(buffer[rows, :])
        high[rows, :] = block_high
        low[rows, :] = block_low
        product[rows, :] = fold(dot(block_high, wide[...]) + dot(block_low, wide[...]))
        return carry

    lax.fori_loop(0, NCHUNK, chunk, 0)
    cut(scalars, product, pieces)


def in_hbm(*arrays):
    return [pltpu.with_memory_space_constraint(array, pltpu.HBM) for array in arrays]


def first_apply(face_start, face_len, operator, vectors):
    half = jax.ShapeDtypeStruct((M, M), bf16)
    return pl.pallas_call(
        first_kernel,
        out_shape=[half, half, VEC, PADDED]
        + [PIECE] * 6
        + [jax.ShapeDtypeStruct((36,), jnp.int32), PAIR],
        in_specs=[HBM] * 4,
        out_specs=[VMEM] * 10 + [SMEM] * 2,
        scratch_shapes=[
            pltpu.VMEM((M, M), f32),
            pltpu.VMEM((LOADS, M), f32),
            pltpu.SMEM((6,), jnp.int32),
            pltpu.SMEM((6,), jnp.int32),
            pltpu.VMEM((M, 2 * LOADS), bf16),
            pltpu.SemaphoreType.DMA((NCHUNK + 3,)),
        ],
        compiler_params=params(20),
        name="first",
    )(*in_hbm(face_start, face_len, operator, vectors))


def turn_kernel(scalars, data, weight, modes, inverse, *rest):
    (data_t, weight_t, modes_rows, modes_t, modes_wide), blocks, scratch = (
        rest[:5],
        rest[5:13],
        rest[13:],
    )
    data_buf, weight_buf, modes_buf, inverse_buf, sems = scratch
    copies = []
    for source, target in (
        (weight, weight_buf), (modes, modes_buf), (data, data_buf), (inverse, inverse_buf)
    ):
        copy = pltpu.make_async_copy(source, target, sems.at[len(copies)])
        copy.start()
        copies.append(copy)
    for copy in copies[:3]:
        copy.wait()

    def strip(k, carry):
        span = pl.ds(pl.multiple_of(k * STRIP, STRIP), STRIP)
        data_t[span, :] = data_buf[:, span].T
        weights = 1.0 / weight_buf[:, span].astype(f32)
        weight_t[span, :] = jnp.broadcast_to(weights, (LOADS, STRIP)).T
        high, low = split(modes_buf[:, span])
        modes_rows[:, span] = jnp.concatenate([high, low], axis=0)
        turned = modes_buf[:, span].T
        high, low = split(turned)
        modes_t[span, :] = jnp.concatenate([high, low, high], axis=1)
        modes_wide[span, :] = jnp.concatenate([turned, jnp.zeros_like(turned)], axis=1)
        return carry

    lax.fori_loop(0, M // STRIP, strip, 0)
    copies[3].wait()
    for mask in range(8):
        for half in range(2):
            offset = pl.multiple_of(scalars[28 + mask] + half * 4096, 512)
            blocks[mask][:, pl.ds(half * 512, 512)] = inverse_buf[:, pl.ds(offset, 512)]


def turn(scalars, data, weight, modes, inverse):
    return pl.pallas_call(
        turn_kernel,
        out_shape=[
            VEC,
            VEC,
            jax.ShapeDtypeStruct((2 * NM, M), bf16),
            jax.ShapeDtypeStruct((M, 3 * NM), bf16),
            VEC,
        ]
        + [jax.ShapeDtypeStruct((NM, 1024), f32)] * 8,
        in_specs=[SMEM] + [HBM] * 4,
        out_specs=[VMEM] * 13,
        scratch_shapes=[
            pltpu.VMEM((LOADS, M), f32),
            pltpu.VMEM((1, M), jnp.int32),
            pltpu.VMEM((NM, M), f32),
            pltpu.VMEM((NM, 8192), f32),
            pltpu.SemaphoreType.DMA((4,)),
        ],
        compiler_params=params(8),
        name="turn",
    )(scalars, *in_hbm(data, weight, modes, inverse))


def step_kernel(
    scalars, gains, high, low, product, weight, residual, correction, multipliers, *rest
):
    received, outs, scratch = rest[:6], rest[6:17], rest[17:]
    new_residual, new_correction, new_multipliers, new_product = outs[:4]
    new_gains = outs[10]
    wide, padded = scratch
    applied = place(scalars, product, received, padded) * weight[...]
    remaining = residual[...] - applied
    new_residual[...] = remaining
    step = gains[0] * correction[...] + gains[1] * remaining
    new_correction[...] = step
    new_multipliers[...] = multipliers[...] + step
    wide[...] = side_by_side(step)
    apply_operator(high, low, wide, new_product)
    cut(scalars, new_product, outs[4:10])
    new_gains[0], new_gains[1] = GAINS[0]


def step(scalars, gains, high, low, product, weight, residual, correction, multipliers, received):
    return pl.pallas_call(
        step_kernel,
        out_shape=[VEC] * 3 + [PADDED] + [PIECE] * 6 + [PAIR],
        in_specs=[SMEM, SMEM] + [VMEM] * 13,
        out_specs=[VMEM] * 10 + [SMEM],
        scratch_shapes=OPERATOR_SCRATCH,
        compiler_params=params(8),
        name="step",
    )(
        scalars, gains, high, low, product, weight, residual, correction, multipliers, *received
    )


def last_kernel(
    scale, gain, scalars, modes, product, weight, residual, correction, multipliers, *rest
):
    received, (new_multipliers, coeffs, padded) = rest[:6], rest[6:]
    applied = place(scalars, product, received, padded) * weight[...]
    remaining = residual[...] - applied
    step = scale * correction[...] + gain * remaining
    moved = multipliers[...] + step
    new_multipliers[...] = moved
    both = dot(modes[...], side_by_side(moved))
    coeffs[...] = fold(both[:NM] + both[NM:])


def last_step(
    scale, gain, scalars, modes, product, weight, residual, correction, multipliers, received
):
    return pl.pallas_call(
        functools.partial(last_kernel, scale, gain),
        out_shape=[VEC, COEF],
        in_specs=[SMEM] + [VMEM] * 12,
        out_specs=[VMEM] * 2,
        scratch_shapes=[pltpu.VMEM((M + PCAP, LOADS), f32)],
        compiler_params=params(8),
        name="last",
    )(scalars, modes, product, weight, residual, correction, multipliers, *received)


def join_kernel(*refs):
    out = refs[-1]
    for k, ref in enumerate(refs[:-1]):
        out[pl.ds(k * NM, NM), :] = ref[...]


def join(pieces):
    return pl.pallas_call(
        join_kernel,
        out_shape=jax.ShapeDtypeStruct((len(pieces) * NM, LOADS), f32),
        in_specs=[VMEM] * len(pieces),
        out_specs=VMEM,
        compiler_params=params(4),
        name="join",
    )(*pieces)


def blocks_kernel(*refs):
    out = refs[-1]
    for mask, block in enumerate(refs[:-1]):
        high, low = split(block[...])
        out[pl.ds(mask * NM, NM), :] = high
        out[pl.ds((8 + mask) * NM, NM), :] = low


def prepare_blocks(blocks):
    return pl.pallas_call(
        blocks_kernel,
        out_shape=jax.ShapeDtypeStruct((16 * NM, 16 * NM), bf16),
        in_specs=[VMEM] * 8,
        out_specs=VMEM,
        compiler_params=params(8),
        name="blocks",
    )(*blocks)


def coarse_kernel(scalars, blocks, *rest):
    gathered, parts, scratch = rest[:4], rest[4:8], rest[8]
    for group in range(4):
        for item in range(4):
            slot = scalars[12 + group * 4 + item]
            rows = pl.ds(pl.multiple_of(slot * NM, NM), NM)
            scratch[rows, :] = side_by_side(gathered[group][pl.ds(item * NM, NM), :])
    half = 8 * NM
    both = dot(blocks[pl.ds(0, half), :], scratch[...])
    both = fold(both + dot(blocks[pl.ds(half, half), :], scratch[...]))
    for mask in range(8):
        parts[mask % 4][pl.ds(mask // 4 * NM, NM), :] = both[mask * NM : (mask + 1) * NM]


def coarse_product(scalars, blocks, gathered):
    return pl.pallas_call(
        coarse_kernel,
        out_shape=[jax.ShapeDtypeStruct((2 * NM, LOADS), f32)] * 4,
        in_specs=[SMEM] + [VMEM] * 5,
        out_specs=[VMEM] * 4,
        scratch_shapes=[pltpu.VMEM((16 * NM, 2 * LOADS), bf16)],
        compiler_params=params(8),
        name="coarse",
    )(scalars, blocks, *gathered)


def sum_kernel(*refs):
    parts, (kept, sent) = refs[:4], refs[4:]
    kept[...] = sum(part[pl.ds(0, NM), :] for part in parts[1:]) + parts[0][pl.ds(0, NM), :]
    sent[...] = sum(part[pl.ds(NM, NM), :] for part in parts[1:]) + parts[0][pl.ds(NM, NM), :]


def sum_parts(parts):
    return pl.pallas_call(
        sum_kernel,
        out_shape=[COEF] * 2,
        in_specs=[VMEM] * 4,
        out_specs=[VMEM] * 2,
        compiler_params=params(4),
        name="sum",
    )(*parts)


def apply_kernel(high, low, vectors, product, wide):
    wide[...] = side_by_side(vectors[...])

    def chunk(k, carry):
        rows = pl.ds(pl.multiple_of(k * WIDE_CHUNK, WIDE_CHUNK), WIDE_CHUNK)
        product[rows, :] = fold(dot(high[rows, :], wide[...]) + dot(low[rows, :], wide[...]))
        return carry

    lax.fori_loop(0, M // WIDE_CHUNK, chunk, 0)


def apply_alone(high, low, vectors):
    return pl.pallas_call(
        apply_kernel,
        out_shape=VEC,
        in_specs=[VMEM] * 3,
        out_specs=VMEM,
        scratch_shapes=OPERATOR_SCRATCH[:1],
        compiler_params=params(8),
        name="apply",
    )(high, low, vectors)


def project_kernel(scalars, modes_t, applied_modes, applied, multipliers, kept, partner, *rest):
    (new_multipliers, product), pieces, gains = rest[:2], rest[2:8], rest[8]
    gains[0], gains[1] = 0.0, 1.0 / center
    amplitude = kept[...] + partner[...]
    amp_high, amp_low = split(amplitude)
    stacked = jnp.concatenate([amp_high, amp_high, amp_low], axis=0)
    both = jnp.concatenate([amp_high, amp_low], axis=1)
    modes_high, modes_low = split(applied_modes[:, pl.ds(0, NM)])
    removed = fold(dot(modes_high, both)) + dot(modes_low, amp_high)
    product[pl.ds(0, M), :] = applied[...] - removed
    product[pl.ds(M, PCAP), :] = jnp.zeros((PCAP, LOADS), f32)
    cut(scalars, product, pieces)
    new_multipliers[...] = multipliers[...] - dot(modes_t[...], stacked)


def project_step(scalars, modes_t, applied_modes, applied, multipliers, kept, partner):
    return pl.pallas_call(
        project_kernel,
        out_shape=[VEC, PADDED] + [PIECE] * 6 + [PAIR],
        in_specs=[SMEM] + [VMEM] * 6,
        out_specs=[VMEM] * 8 + [SMEM],
        compiler_params=params(8),
        name="project",
    )(scalars, modes_t, applied_modes, applied, multipliers, kept, partner)


def emit_kernel(vectors, out):
    out[...] = vectors[...].T


def emit(vectors):
    return pl.pallas_call(
        emit_kernel,
        out_shape=jax.ShapeDtypeStruct((LOADS, M), f32),
        in_specs=[VMEM],
        out_specs=VMEM,
        compiler_params=params(8),
        name="emit",
    )(vectors)


def final_kernel(scalars, product, weight, data, *rest):
    received, (residual_out, padded) = rest[:6], rest[6:]
    applied = place(scalars, product, received, padded) * weight[...]
    residual_out[...] = (data[...] - applied).T


def final_step(scalars, product, weight, data, received):
    return pl.pallas_call(
        final_kernel,
        out_shape=jax.ShapeDtypeStruct((LOADS, M), f32),
        in_specs=[SMEM] + [VMEM] * 9,
        out_specs=VMEM,
        scratch_shapes=[pltpu.VMEM((M + PCAP, LOADS), f32)],
        compiler_params=params(8),
        name="final",
    )(scalars, product, weight, data, *received)


def swap_pairs(count, odd):
    lower = range(odd, count, 2)
    pairs = [(i, (i + 1) % count) for i in lower]
    return pairs + [(target, source) for source, target in pairs]


def exchange(pieces):
    received = []
    for piece, (number, kind) in zip(pieces, SLOTS):
        axes = (GX, GY, GZ)[number]
        received.append(lax.ppermute(piece, axes, swap_pairs(lax.axis_size(axes), kind)))
    return received


def xor_pairs(count, mask):
    return [(i, i ^ mask) for i in range(count)]


def per_device(
    load_data,
    initial_dual,
    dual_operator,
    coarse_modes,
    coarse_inverse,
    face_start,
    face_len,
    multiplicity,
):
    def gather(coeffs):
        line = join(
            [coeffs]
            + [lax.ppermute(coeffs, ("xh", "xl"), xor_pairs(4, mask)) for mask in range(1, 4)]
        )
        return [line] + [lax.ppermute(line, "y", xor_pairs(4, mask)) for mask in range(1, 4)]

    def scatter(parts, beside):
        parts = [parts[0]] + [
            lax.ppermute(parts[mask], "gy", xor_pairs(4, mask)) for mask in range(1, 4)
        ]
        parts, beside = lax.optimization_barrier((parts, beside))
        kept, sent = sum_parts(parts)
        return beside, kept, lax.ppermute(sent, "co", xor_pairs(2, 1))

    high, low, multipliers, product, *pieces, scalars, gains = first_apply(
        face_start[0, 0, 0], face_len[0, 0, 0], dual_operator[0, 0, 0], initial_dual[0, 0, 0]
    )
    data, weight, modes_rows, modes_t, modes_wide, *blocks = turn(
        scalars, load_data[0, 0, 0], multiplicity[0, 0], coarse_modes[0, 0, 0], coarse_inverse
    )

    def move_blocks(received, masks):
        for mask in masks:
            blocks[mask] = lax.ppermute(blocks[mask], RSG, xor_pairs(8, mask))
        moved = [blocks[mask] for mask in masks]
        received, moved = lax.optimization_barrier((received, moved))
        for mask, block in zip(masks, moved):
            blocks[mask] = block
        return received

    received = exchange(pieces)
    for outer in range(OUTER):
        residual = correction = data
        for index in range(CHEB - 1):
            if outer == 0:
                received = move_blocks(received, WINDOWS[index])
            residual, correction, multipliers, product, *pieces, gains = step(
                scalars, gains, high, low, product, weight,
                residual, correction, multipliers, received,
            )
            if outer == 0 and index == 0:
                modes_wide, residual = lax.optimization_barrier((modes_wide, residual))
                applied_modes = apply_alone(high, low, modes_wide)
            received = exchange(pieces)
        if outer == 0:
            received = move_blocks(received, WINDOWS[-1])
            for mask in (1, 3):
                blocks[mask] = lax.ppermute(blocks[mask], RSG, xor_pairs(8, mask))
            prepared = prepare_blocks(blocks)
        multipliers, coeffs = last_step(
            *GAINS[-1], scalars, modes_rows, product, weight,
            residual, correction, multipliers, received,
        )
        applied = apply_alone(high, low, multipliers)
        gathered, applied = lax.optimization_barrier((gather(coeffs), applied))
        applied_modes, kept, partner = scatter(
            coarse_product(scalars, prepared, gathered), applied_modes
        )
        multipliers, product, *pieces, gains = project_step(
            scalars, modes_t, applied_modes, applied, multipliers, kept, partner
        )
        received = exchange(pieces)
    solved = emit(multipliers)
    final_residual = final_step(scalars, product, weight, data, received)
    return solved.reshape(initial_dual.shape), final_residual.reshape(initial_dual.shape)


def solution(mesh):
    fine = Mesh(mesh.devices.reshape(2, 2, 4, 4, 2), ("xh", "co", "gy", "y", "xl"))
    grid = (GX, "gy", GZ)
    placed = (
        P(*grid, None, None),
        P(*grid, None, None),
        P(*grid, None, None),
        P(*grid, None, None),
        P(("xh", "co", "gy", "y", "xl"), None),
        P(*grid, None),
        P(*grid, None),
        P(*grid, None),
    )
    return jax.shard_map(
        per_device,
        mesh=fine,
        in_specs=placed,
        out_specs=(P(*grid, None, None), P(*grid, None, None)),
        check_vma=False,
    )
```

```python
import functools

import jax
import jax.numpy as jnp
from jax import lax
from jax.experimental import pallas as pl
from jax.experimental.pallas import tpu as pltpu
from jax.sharding import Mesh, PartitionSpec as P

M = 1536
PCAP = 256
NM = 64
LOADS = 128
OUTER = 2
CHEB = 3
CHUNK = 256
NCHUNK = M // CHUNK
STRIP = 1536
WIDE_CHUNK = 512


center = 1.0
half_width = 0.9

f32 = jnp.float32
bf16 = jnp.bfloat16

GX = ("xh", "co")
GY = ("gy",)
GZ = ("y", "xl")
RSG = ("co", "gy")


def recurrence():
    stretch = center / half_width
    rho = 1.0 / stretch
    gains = []
    for _ in range(CHEB - 1):
        rho_next = 1.0 / (2.0 * stretch - rho)
        gains.append((rho_next * rho, 2.0 * rho_next / half_width))
        rho = rho_next
    return gains


GAINS = recurrence()

VEC = jax.ShapeDtypeStruct((M, LOADS), f32)
PADDED = jax.ShapeDtypeStruct((M + PCAP, LOADS), f32)
PIECE = jax.ShapeDtypeStruct((PCAP, LOADS), f32)
PAIR = jax.ShapeDtypeStruct((2,), f32)
COEF = jax.ShapeDtypeStruct((NM, LOADS), f32)
VMEM = pl.BlockSpec(memory_space=pltpu.VMEM)
SMEM = pl.BlockSpec(memory_space=pltpu.SMEM)
HBM = pl.BlockSpec(memory_space=pltpu.HBM)

WINDOWS = ((), (2, 4, 5), (6, 7))

SLOTS = ((2, 1), (0, 1), (1, 1), (2, 0), (1, 0), (0, 0))


def split(x):
    high = x.astype(bf16)
    return high, (x - high.astype(f32)).astype(bf16)


def side_by_side(x):
    return jnp.concatenate(split(x), axis=1)


def fold(x):
    return x[:, :LOADS] + x[:, LOADS:]


def dot(a, b):
    return lax.dot_general(a, b, (((1,), (0,)), ((), ())), preferred_element_type=f32)


def apply_operator(high, low, wide, padded):
    for k in range(NCHUNK):
        rows = pl.ds(k * CHUNK, CHUNK)
        padded[rows, :] = fold(dot(high[rows, :], wide[...]) + dot(low[rows, :], wide[...]))
    padded[pl.ds(M, PCAP), :] = jnp.zeros((PCAP, LOADS), f32)


def cut(scalars, padded, pieces):
    for face in range(6):
        pieces[face][...] = padded[pl.ds(scalars[face], PCAP), :]


def place(scalars, product, received, padded):
    padded[pl.ds(0, M), :] = product[pl.ds(0, M), :]
    row = lax.broadcasted_iota(jnp.int32, (PCAP, LOADS), 0)
    for face in range(6):
        window = pl.ds(scalars[face], PCAP)
        padded[window, :] = padded[window, :] + jnp.where(
            row < scalars[6 + face], received[face][...], 0.0
        )
    return padded[pl.ds(0, M), :]


OPERATOR_SCRATCH = [
    pltpu.VMEM((M, 2 * LOADS), bf16),
    pltpu.VMEM((M + PCAP, LOADS), f32),
]


def params(megabytes):
    return pltpu.CompilerParams(vmem_limit_bytes=megabytes << 20)


def axis_position(axes):
    position = 0
    for name in axes:
        position = position * lax.axis_size(name) + lax.axis_index(name)
    return position


def first_kernel(start_in, len_in, operator, vectors, *rest):
    (high, low, vectors_t, product), pieces, scratch = rest[:4], rest[4:10], rest[13:]
    scalars, start_gains, inner_gains = rest[10:13]
    start_gains[0], start_gains[1] = 0.0, 1.0 / center
    inner_gains[0], inner_gains[1] = GAINS[0]
    buffer, vector_buf, face_start, face_len, wide, sems = scratch

    def chunk_copy(k):
        rows = pl.ds(pl.multiple_of(k * CHUNK, CHUNK), CHUNK)
        return pltpu.make_async_copy(operator.at[rows], buffer.at[rows], sems.at[k])

    small = []
    for source, target in ((start_in, face_start), (len_in, face_len), (vectors, vector_buf)):
        copy = pltpu.make_async_copy(source, target, sems.at[NCHUNK + len(small)])
        copy.start()
        small.append(copy)
    for k in range(NCHUNK):
        chunk_copy(k).start()
    small[0].wait()
    small[1].wait()
    for slot, (number, kind) in enumerate(SLOTS):
        axes = (GX, GY, GZ)[number]
        position = axis_position(axes)
        count = lax.axis_size(axes)
        parity = position & 1
        face = 2 * number + (parity if kind else 1 - parity)
        length = face_len[face]
        if kind:
            length = jnp.where((position > 0) & (position < count - 1), length, 0)
        scalars[slot] = face_start[face]
        scalars[6 + slot] = length
    along_x = axis_position(("xh", "xl"))
    along_y = axis_position(("y",))
    for y_mask in range(4):
        for x_mask in range(4):
            x = along_x ^ x_mask
            scalars[12 + y_mask * 4 + x_mask] = (
                (x >> 1) * 8 + (along_y ^ y_mask) * 2 + (x & 1)
            )
    group = axis_position(RSG)
    for mask in range(8):
        scalars[28 + mask] = (group ^ mask) * 512
    small[2].wait()
    turned = vector_buf[...].T
    vectors_t[...] = turned
    wide[...] = side_by_side(turned)
    product[pl.ds(M, PCAP), :] = jnp.zeros((PCAP, LOADS), f32)

    def chunk(k, carry):
        chunk_copy(k).wait()
        rows = pl.ds(pl.multiple_of(k * CHUNK, CHUNK), CHUNK)
        block_high, block_low = split(buffer[rows, :])
        high[rows, :] = block_high
        low[rows, :] = block_low
        product[rows, :] = fold(dot(block_high, wide[...]) + dot(block_low, wide[...]))
        return carry

    lax.fori_loop(0, NCHUNK, chunk, 0)
    cut(scalars, product, pieces)


def in_hbm(*arrays):
    return [pltpu.with_memory_space_constraint(array, pltpu.HBM) for array in arrays]


def first_apply(face_start, face_len, operator, vectors):
    half = jax.ShapeDtypeStruct((M, M), bf16)
    return pl.pallas_call(
        first_kernel,
        out_shape=[half, half, VEC, PADDED]
        + [PIECE] * 6
        + [jax.ShapeDtypeStruct((36,), jnp.int32), PAIR, PAIR],
        in_specs=[HBM] * 4,
        out_specs=[VMEM] * 10 + [SMEM] * 3,
        scratch_shapes=[
            pltpu.VMEM((M, M), f32),
            pltpu.VMEM((LOADS, M), f32),
            pltpu.SMEM((6,), jnp.int32),
            pltpu.SMEM((6,), jnp.int32),
            pltpu.VMEM((M, 2 * LOADS), bf16),
            pltpu.SemaphoreType.DMA((NCHUNK + 3,)),
        ],
        compiler_params=params(20),
        name="first",
    )(*in_hbm(face_start, face_len, operator, vectors))


def turn_kernel(scalars, data, weight, modes, inverse, *rest):
    (data_t, weight_t, modes_rows, modes_t, modes_wide), blocks, scratch = (
        rest[:5],
        rest[5:13],
        rest[13:],
    )
    data_buf, weight_buf, modes_buf, inverse_buf, sems = scratch
    copies = []
    for source, target in (
        (weight, weight_buf), (modes, modes_buf), (data, data_buf), (inverse, inverse_buf)
    ):
        copy = pltpu.make_async_copy(source, target, sems.at[len(copies)])
        copy.start()
        copies.append(copy)
    for copy in copies[:3]:
        copy.wait()

    def strip(k, carry):
        span = pl.ds(pl.multiple_of(k * STRIP, STRIP), STRIP)
        data_t[span, :] = data_buf[:, span].T
        weights = 1.0 / weight_buf[:, span].astype(f32)
        weight_t[span, :] = jnp.broadcast_to(weights, (LOADS, STRIP)).T
        high, low = split(modes_buf[:, span])
        modes_rows[:, span] = jnp.concatenate([high, low], axis=0)
        turned = modes_buf[:, span].T
        high, low = split(turned)
        modes_t[span, :] = jnp.concatenate([high, low, high], axis=1)
        modes_wide[span, :] = jnp.concatenate([turned, jnp.zeros_like(turned)], axis=1)
        return carry

    lax.fori_loop(0, M // STRIP, strip, 0)
    copies[3].wait()
    for mask in range(8):
        for half in range(2):
            offset = pl.multiple_of(scalars[28 + mask] + half * 4096, 512)
            blocks[mask][:, pl.ds(half * 512, 512)] = inverse_buf[:, pl.ds(offset, 512)]


def turn(scalars, data, weight, modes, inverse):
    return pl.pallas_call(
        turn_kernel,
        out_shape=[
            VEC,
            VEC,
            jax.ShapeDtypeStruct((2 * NM, M), bf16),
            jax.ShapeDtypeStruct((M, 3 * NM), bf16),
            VEC,
        ]
        + [jax.ShapeDtypeStruct((NM, 1024), f32)] * 8,
        in_specs=[SMEM] + [HBM] * 4,
        out_specs=[VMEM] * 13,
        scratch_shapes=[
            pltpu.VMEM((LOADS, M), f32),
            pltpu.VMEM((1, M), jnp.int32),
            pltpu.VMEM((NM, M), f32),
            pltpu.VMEM((NM, 8192), f32),
            pltpu.SemaphoreType.DMA((4,)),
        ],
        compiler_params=params(8),
        name="turn",
    )(scalars, *in_hbm(data, weight, modes, inverse))


def step_kernel(
    scalars, gains, high, low, product, weight, residual, correction, multipliers, *rest
):
    received, outs, scratch = rest[:6], rest[6:16], rest[16:]
    new_residual, new_correction, new_multipliers, new_product = outs[:4]
    wide, padded = scratch
    applied = place(scalars, product, received, padded) * weight[...]
    remaining = residual[...] - applied
    new_residual[...] = remaining
    step = gains[0] * correction[...] + gains[1] * remaining
    new_correction[...] = step
    new_multipliers[...] = multipliers[...] + step
    wide[...] = side_by_side(step)
    apply_operator(high, low, wide, new_product)
    cut(scalars, new_product, outs[4:])


def step(scalars, gains, high, low, product, weight, residual, correction, multipliers, received):
    return pl.pallas_call(
        step_kernel,
        out_shape=[VEC] * 3 + [PADDED] + [PIECE] * 6,
        in_specs=[SMEM, SMEM] + [VMEM] * 13,
        out_specs=[VMEM] * 10,
        scratch_shapes=OPERATOR_SCRATCH,
        compiler_params=params(8),
        name="step",
    )(
        scalars, gains, high, low, product, weight, residual, correction, multipliers, *received
    )


def last_kernel(
    scale, gain, scalars, modes, product, weight, residual, correction, multipliers, *rest
):
    received, (new_multipliers, coeffs, padded) = rest[:6], rest[6:]
    applied = place(scalars, product, received, padded) * weight[...]
    remaining = residual[...] - applied
    step = scale * correction[...] + gain * remaining
    moved = multipliers[...] + step
    new_multipliers[...] = moved
    both = dot(modes[...], side_by_side(moved))
    coeffs[...] = fold(both[:NM] + both[NM:])


def last_step(
    scale, gain, scalars, modes, product, weight, residual, correction, multipliers, received
):
    return pl.pallas_call(
        functools.partial(last_kernel, scale, gain),
        out_shape=[VEC, COEF],
        in_specs=[SMEM] + [VMEM] * 12,
        out_specs=[VMEM] * 2,
        scratch_shapes=[pltpu.VMEM((M + PCAP, LOADS), f32)],
        compiler_params=params(8),
        name="last",
    )(scalars, modes, product, weight, residual, correction, multipliers, *received)


def join_kernel(*refs):
    out = refs[-1]
    for k, ref in enumerate(refs[:-1]):
        out[pl.ds(k * NM, NM), :] = ref[...]


def join(pieces):
    return pl.pallas_call(
        join_kernel,
        out_shape=jax.ShapeDtypeStruct((len(pieces) * NM, LOADS), f32),
        in_specs=[VMEM] * len(pieces),
        out_specs=VMEM,
        compiler_params=params(4),
        name="join",
    )(*pieces)


def blocks_kernel(*refs):
    out = refs[-1]
    for mask, block in enumerate(refs[:-1]):
        high, low = split(block[...])
        out[pl.ds(mask * NM, NM), :] = high
        out[pl.ds((8 + mask) * NM, NM), :] = low


def prepare_blocks(blocks):
    return pl.pallas_call(
        blocks_kernel,
        out_shape=jax.ShapeDtypeStruct((16 * NM, 16 * NM), bf16),
        in_specs=[VMEM] * 8,
        out_specs=VMEM,
        compiler_params=params(8),
        name="blocks",
    )(*blocks)


def coarse_kernel(scalars, blocks, *rest):
    gathered, parts, scratch = rest[:4], rest[4:6], rest[6]
    for group in range(4):
        for item in range(4):
            slot = scalars[12 + group * 4 + item]
            rows = pl.ds(pl.multiple_of(slot * NM, NM), NM)
            scratch[rows, :] = side_by_side(gathered[group][pl.ds(item * NM, NM), :])
    half = 8 * NM
    both = dot(blocks[pl.ds(0, half), :], scratch[...])
    both = fold(both + dot(blocks[pl.ds(half, half), :], scratch[...]))
    parts[0][...] = both[: 4 * NM]
    parts[1][...] = both[4 * NM :]


def coarse_product(scalars, blocks, gathered):
    return pl.pallas_call(
        coarse_kernel,
        out_shape=[jax.ShapeDtypeStruct((4 * NM, LOADS), f32)] * 2,
        in_specs=[SMEM] + [VMEM] * 5,
        out_specs=[VMEM] * 2,
        scratch_shapes=[pltpu.VMEM((16 * NM, 2 * LOADS), bf16)],
        compiler_params=params(8),
        name="coarse",
    )(scalars, blocks, *gathered)


def sum_kernel(kept, partner, *parts):
    for k, part in enumerate(parts):
        rows = pl.ds(k * NM, NM)
        part[...] = kept[rows, :] + partner[rows, :]


def sum_parts(kept, partner):
    return pl.pallas_call(
        sum_kernel,
        out_shape=[COEF] * 4,
        in_specs=[VMEM] * 2,
        out_specs=[VMEM] * 4,
        compiler_params=params(4),
        name="sum",
    )(kept, partner)


def apply_kernel(high, low, vectors, product, wide):
    wide[...] = side_by_side(vectors[...])

    def chunk(k, carry):
        rows = pl.ds(pl.multiple_of(k * WIDE_CHUNK, WIDE_CHUNK), WIDE_CHUNK)
        product[rows, :] = fold(dot(high[rows, :], wide[...]) + dot(low[rows, :], wide[...]))
        return carry

    lax.fori_loop(0, M // WIDE_CHUNK, chunk, 0)


def apply_alone(high, low, vectors):
    return pl.pallas_call(
        apply_kernel,
        out_shape=VEC,
        in_specs=[VMEM] * 3,
        out_specs=VMEM,
        scratch_shapes=OPERATOR_SCRATCH[:1],
        compiler_params=params(8),
        name="apply",
    )(high, low, vectors)


def project_kernel(scalars, modes_t, applied_modes, applied, multipliers, *rest):
    parts, (new_multipliers, product), pieces = rest[:4], rest[4:6], rest[6:12]
    amplitude = (parts[0][...] + parts[1][...]) + (parts[2][...] + parts[3][...])
    amp_high, amp_low = split(amplitude)
    stacked = jnp.concatenate([amp_high, amp_high, amp_low], axis=0)
    both = jnp.concatenate([amp_high, amp_low], axis=1)
    modes_high, modes_low = split(applied_modes[:, pl.ds(0, NM)])
    removed = fold(dot(modes_high, both)) + dot(modes_low, amp_high)
    product[pl.ds(0, M), :] = applied[...] - removed
    product[pl.ds(M, PCAP), :] = jnp.zeros((PCAP, LOADS), f32)
    cut(scalars, product, pieces)
    new_multipliers[...] = multipliers[...] - dot(modes_t[...], stacked)


def project_step(scalars, modes_t, applied_modes, applied, multipliers, parts):
    return pl.pallas_call(
        project_kernel,
        out_shape=[VEC, PADDED] + [PIECE] * 6,
        in_specs=[SMEM] + [VMEM] * 8,
        out_specs=[VMEM] * 8,
        compiler_params=params(8),
        name="project",
    )(scalars, modes_t, applied_modes, applied, multipliers, *parts)


def emit_kernel(vectors, out):
    out[...] = vectors[...].T


def emit(vectors):
    return pl.pallas_call(
        emit_kernel,
        out_shape=jax.ShapeDtypeStruct((LOADS, M), f32),
        in_specs=[VMEM],
        out_specs=VMEM,
        compiler_params=params(8),
        name="emit",
    )(vectors)


def final_kernel(scalars, product, weight, data, *rest):
    received, (residual_out, padded) = rest[:6], rest[6:]
    applied = place(scalars, product, received, padded) * weight[...]
    residual_out[...] = (data[...] - applied).T


def final_step(scalars, product, weight, data, received):
    return pl.pallas_call(
        final_kernel,
        out_shape=jax.ShapeDtypeStruct((LOADS, M), f32),
        in_specs=[SMEM] + [VMEM] * 9,
        out_specs=VMEM,
        scratch_shapes=[pltpu.VMEM((M + PCAP, LOADS), f32)],
        compiler_params=params(8),
        name="final",
    )(scalars, product, weight, data, *received)


def swap_pairs(count, odd):
    lower = range(odd, count, 2)
    pairs = [(i, (i + 1) % count) for i in lower]
    return pairs + [(target, source) for source, target in pairs]


def exchange(pieces):
    received = []
    for piece, (number, kind) in zip(pieces, SLOTS):
        axes = (GX, GY, GZ)[number]
        received.append(lax.ppermute(piece, axes, swap_pairs(lax.axis_size(axes), kind)))
    return received


def xor_pairs(count, mask):
    return [(i, i ^ mask) for i in range(count)]


def per_device(
    load_data,
    initial_dual,
    dual_operator,
    coarse_modes,
    coarse_inverse,
    face_start,
    face_len,
    multiplicity,
):
    def gather(coeffs):
        line = join(
            [coeffs]
            + [lax.ppermute(coeffs, ("xh", "xl"), xor_pairs(4, mask)) for mask in range(1, 4)]
        )
        return [line] + [lax.ppermute(line, "y", xor_pairs(4, mask)) for mask in range(1, 4)]

    def scatter(kept, sent, beside):
        parts = sum_parts(kept, lax.ppermute(sent, "co", xor_pairs(2, 1)))
        parts = [parts[0]] + [
            lax.ppermute(parts[mask], "gy", xor_pairs(4, mask)) for mask in range(1, 4)
        ]
        return lax.optimization_barrier((parts, beside))

    high, low, multipliers, product, *pieces, scalars, start_gains, inner_gains = first_apply(
        face_start[0, 0, 0], face_len[0, 0, 0], dual_operator[0, 0, 0], initial_dual[0, 0, 0]
    )
    data, weight, modes_rows, modes_t, modes_wide, *blocks = turn(
        scalars, load_data[0, 0, 0], multiplicity[0, 0], coarse_modes[0, 0, 0], coarse_inverse
    )

    def move_blocks(received, masks):
        for mask in masks:
            blocks[mask] = lax.ppermute(blocks[mask], RSG, xor_pairs(8, mask))
        moved = [blocks[mask] for mask in masks]
        received, moved = lax.optimization_barrier((received, moved))
        for mask, block in zip(masks, moved):
            blocks[mask] = block
        return received

    received = exchange(pieces)
    for outer in range(OUTER):
        residual = correction = data
        for index in range(CHEB - 1):
            if outer == 0:
                received = move_blocks(received, WINDOWS[index])
            residual, correction, multipliers, product, *pieces = step(
                scalars, inner_gains if index else start_gains, high, low, product, weight,
                residual, correction, multipliers, received,
            )
            if outer == 0 and index == 0:
                modes_wide, residual = lax.optimization_barrier((modes_wide, residual))
                applied_modes = apply_alone(high, low, modes_wide)
            received = exchange(pieces)
        if outer == 0:
            received = move_blocks(received, WINDOWS[-1])
            for mask in (1, 3):
                blocks[mask] = lax.ppermute(blocks[mask], RSG, xor_pairs(8, mask))
            prepared = prepare_blocks(blocks)
        multipliers, coeffs = last_step(
            *GAINS[-1], scalars, modes_rows, product, weight,
            residual, correction, multipliers, received,
        )
        applied = apply_alone(high, low, multipliers)
        gathered, applied = lax.optimization_barrier((gather(coeffs), applied))
        parts, applied_modes = scatter(
            *coarse_product(scalars, prepared, gathered), applied_modes
        )
        multipliers, product, *pieces = project_step(
            scalars, modes_t, applied_modes, applied, multipliers, parts
        )
        received = exchange(pieces)
    solved = emit(multipliers)
    final_residual = final_step(scalars, product, weight, data, received)
    return solved.reshape(initial_dual.shape), final_residual.reshape(initial_dual.shape)


def solution(mesh):
    fine = Mesh(mesh.devices.reshape(2, 2, 4, 4, 2), ("xh", "co", "gy", "y", "xl"))
    grid = (GX, "gy", GZ)
    placed = (
        P(*grid, None, None),
        P(*grid, None, None),
        P(*grid, None, None),
        P(*grid, None, None),
        P(("xh", "co", "gy", "y", "xl"), None),
        P(*grid, None),
        P(*grid, None),
        P(*grid, None),
    )
    return jax.shard_map(
        per_device,
        mesh=fine,
        in_specs=placed,
        out_specs=(P(*grid, None, None), P(*grid, None, None)),
        check_vma=False,
    )
```

```python
import functools

import jax
import jax.numpy as jnp
from jax import lax
from jax.experimental import pallas as pl
from jax.experimental.pallas import tpu as pltpu
from jax.sharding import Mesh, PartitionSpec as P

M = 1536
PCAP = 256
NM = 64
LOADS = 128
OUTER = 2
CHEB = 3
CHUNK = 256
NCHUNK = M // CHUNK
STRIP = 1536
WIDE_CHUNK = 512


center = 1.0
half_width = 0.9

f32 = jnp.float32
bf16 = jnp.bfloat16

GX = ("xh", "co")
GY = ("gy",)
GZ = ("y", "xl")
RSG = ("co", "gy")


def recurrence():
    stretch = center / half_width
    rho = 1.0 / stretch
    gains = []
    for _ in range(CHEB - 1):
        rho_next = 1.0 / (2.0 * stretch - rho)
        gains.append((rho_next * rho, 2.0 * rho_next / half_width))
        rho = rho_next
    return gains


GAINS = recurrence()

VEC = jax.ShapeDtypeStruct((M, LOADS), f32)
PADDED = jax.ShapeDtypeStruct((M + PCAP, LOADS), f32)
PIECE = jax.ShapeDtypeStruct((PCAP, LOADS), f32)
PAIR = jax.ShapeDtypeStruct((2,), f32)
COEF = jax.ShapeDtypeStruct((NM, LOADS), f32)
VMEM = pl.BlockSpec(memory_space=pltpu.VMEM)
SMEM = pl.BlockSpec(memory_space=pltpu.SMEM)
HBM = pl.BlockSpec(memory_space=pltpu.HBM)

WINDOWS = ((), (2, 4, 5), (6, 7))

SLOTS = ((2, 1), (0, 1), (1, 1), (2, 0), (1, 0), (0, 0))


def split(x):
    high = x.astype(bf16)
    return high, (x - high.astype(f32)).astype(bf16)


def side_by_side(x):
    return jnp.concatenate(split(x), axis=1)


def fold(x):
    return x[:, :LOADS] + x[:, LOADS:]


def dot(a, b):
    return lax.dot_general(a, b, (((1,), (0,)), ((), ())), preferred_element_type=f32)


def apply_operator(high, low, wide, padded):
    for k in range(NCHUNK):
        rows = pl.ds(k * CHUNK, CHUNK)
        padded[rows, :] = fold(dot(high[rows, :], wide[...]) + dot(low[rows, :], wide[...]))
    padded[pl.ds(M, PCAP), :] = jnp.zeros((PCAP, LOADS), f32)


def cut(scalars, padded, pieces):
    for face in range(6):
        pieces[face][...] = padded[pl.ds(scalars[face], PCAP), :]


def place(scalars, product, received, padded):
    padded[pl.ds(0, M), :] = product[pl.ds(0, M), :]
    row = lax.broadcasted_iota(jnp.int32, (PCAP, LOADS), 0)
    for face in range(6):
        window = pl.ds(scalars[face], PCAP)
        padded[window, :] = padded[window, :] + jnp.where(
            row < scalars[6 + face], received[face][...], 0.0
        )
    return padded[pl.ds(0, M), :]


OPERATOR_SCRATCH = [
    pltpu.VMEM((M, 2 * LOADS), bf16),
    pltpu.VMEM((M + PCAP, LOADS), f32),
]


def params(megabytes):
    return pltpu.CompilerParams(vmem_limit_bytes=megabytes << 20)


def axis_position(axes):
    position = 0
    for name in axes:
        position = position * lax.axis_size(name) + lax.axis_index(name)
    return position


def first_kernel(start_in, len_in, operator, vectors, *rest):
    (high, low, vectors_t, product), pieces, scratch = rest[:4], rest[4:10], rest[13:]
    scalars, start_gains, inner_gains = rest[10:13]
    start_gains[0], start_gains[1] = 0.0, 1.0 / center
    inner_gains[0], inner_gains[1] = GAINS[0]
    buffer, vector_buf, face_start, face_len, wide, sems = scratch

    def chunk_copy(k):
        rows = pl.ds(pl.multiple_of(k * CHUNK, CHUNK), CHUNK)
        return pltpu.make_async_copy(operator.at[rows], buffer.at[rows], sems.at[k])

    small = []
    for source, target in ((start_in, face_start), (len_in, face_len), (vectors, vector_buf)):
        copy = pltpu.make_async_copy(source, target, sems.at[NCHUNK + len(small)])
        copy.start()
        small.append(copy)
    for k in range(NCHUNK):
        chunk_copy(k).start()
    small[0].wait()
    small[1].wait()
    for slot, (number, kind) in enumerate(SLOTS):
        axes = (GX, GY, GZ)[number]
        position = axis_position(axes)
        count = lax.axis_size(axes)
        parity = position & 1
        face = 2 * number + (parity if kind else 1 - parity)
        length = face_len[face]
        if kind:
            length = jnp.where((position > 0) & (position < count - 1), length, 0)
        scalars[slot] = face_start[face]
        scalars[6 + slot] = length
    along_x = axis_position(("xh", "xl"))
    along_y = axis_position(("y",))
    for y_mask in range(4):
        for x_mask in range(4):
            x = along_x ^ x_mask
            scalars[12 + y_mask * 4 + x_mask] = (
                (x >> 1) * 8 + (along_y ^ y_mask) * 2 + (x & 1)
            )
    group = axis_position(RSG)
    for mask in range(8):
        scalars[28 + mask] = (group ^ mask) * 512
    small[2].wait()
    turned = vector_buf[...].T
    vectors_t[...] = turned
    wide[...] = side_by_side(turned)
    product[pl.ds(M, PCAP), :] = jnp.zeros((PCAP, LOADS), f32)

    def chunk(k, carry):
        chunk_copy(k).wait()
        rows = pl.ds(pl.multiple_of(k * CHUNK, CHUNK), CHUNK)
        block_high, block_low = split(buffer[rows, :])
        high[rows, :] = block_high
        low[rows, :] = block_low
        product[rows, :] = fold(dot(block_high, wide[...]) + dot(block_low, wide[...]))
        return carry

    lax.fori_loop(0, NCHUNK, chunk, 0)
    cut(scalars, product, pieces)


def in_hbm(*arrays):
    return [pltpu.with_memory_space_constraint(array, pltpu.HBM) for array in arrays]


def first_apply(face_start, face_len, operator, vectors):
    half = jax.ShapeDtypeStruct((M, M), bf16)
    return pl.pallas_call(
        first_kernel,
        out_shape=[half, half, VEC, PADDED]
        + [PIECE] * 6
        + [jax.ShapeDtypeStruct((36,), jnp.int32), PAIR, PAIR],
        in_specs=[HBM] * 4,
        out_specs=[VMEM] * 10 + [SMEM] * 3,
        scratch_shapes=[
            pltpu.VMEM((M, M), f32),
            pltpu.VMEM((LOADS, M), f32),
            pltpu.SMEM((6,), jnp.int32),
            pltpu.SMEM((6,), jnp.int32),
            pltpu.VMEM((M, 2 * LOADS), bf16),
            pltpu.SemaphoreType.DMA((NCHUNK + 3,)),
        ],
        compiler_params=params(20),
        name="first",
    )(*in_hbm(face_start, face_len, operator, vectors))


def turn_kernel(scalars, data_buf, weight_buf, modes_buf, inverse_buf, *rest):
    (data_t, weight_t, modes_rows, modes_t, modes_wide), blocks = rest[:5], rest[5:]

    def strip(k, carry):
        span = pl.ds(pl.multiple_of(k * STRIP, STRIP), STRIP)
        data_t[span, :] = data_buf[:, span].T
        weights = 1.0 / weight_buf[:, span].astype(f32)
        weight_t[span, :] = jnp.broadcast_to(weights, (LOADS, STRIP)).T
        high, low = split(modes_buf[:, span])
        modes_rows[:, span] = jnp.concatenate([high, low], axis=0)
        turned = modes_buf[:, span].T
        high, low = split(turned)
        modes_t[span, :] = jnp.concatenate([high, low, high], axis=1)
        modes_wide[span, :] = jnp.concatenate([turned, jnp.zeros_like(turned)], axis=1)
        return carry

    lax.fori_loop(0, M // STRIP, strip, 0)
    for mask in range(8):
        for half in range(2):
            offset = pl.multiple_of(scalars[28 + mask] + half * 4096, 512)
            blocks[mask][:, pl.ds(half * 512, 512)] = inverse_buf[:, pl.ds(offset, 512)]


def turn(scalars, data, weight, modes, inverse):
    return pl.pallas_call(
        turn_kernel,
        out_shape=[
            VEC,
            VEC,
            jax.ShapeDtypeStruct((2 * NM, M), bf16),
            jax.ShapeDtypeStruct((M, 3 * NM), bf16),
            VEC,
        ]
        + [jax.ShapeDtypeStruct((NM, 1024), f32)] * 8,
        in_specs=[SMEM] + [VMEM] * 4,
        out_specs=[VMEM] * 13,
        compiler_params=params(8),
        name="turn",
    )(scalars, data, weight, modes, inverse)


def step_kernel(
    scalars, gains, high, low, product, weight, residual, correction, multipliers, *rest
):
    received, outs, scratch = rest[:6], rest[6:16], rest[16:]
    new_residual, new_correction, new_multipliers, new_product = outs[:4]
    wide, padded = scratch
    applied = place(scalars, product, received, padded) * weight[...]
    remaining = residual[...] - applied
    new_residual[...] = remaining
    step = gains[0] * correction[...] + gains[1] * remaining
    new_correction[...] = step
    new_multipliers[...] = multipliers[...] + step
    wide[...] = side_by_side(step)
    apply_operator(high, low, wide, new_product)
    cut(scalars, new_product, outs[4:])


def step(scalars, gains, high, low, product, weight, residual, correction, multipliers, received):
    return pl.pallas_call(
        step_kernel,
        out_shape=[VEC] * 3 + [PADDED] + [PIECE] * 6,
        in_specs=[SMEM, SMEM] + [VMEM] * 13,
        out_specs=[VMEM] * 10,
        scratch_shapes=OPERATOR_SCRATCH,
        compiler_params=params(8),
        name="step",
    )(
        scalars, gains, high, low, product, weight, residual, correction, multipliers, *received
    )


def last_kernel(
    scale, gain, scalars, modes, product, weight, residual, correction, multipliers, *rest
):
    received, (new_multipliers, coeffs, padded) = rest[:6], rest[6:]
    applied = place(scalars, product, received, padded) * weight[...]
    remaining = residual[...] - applied
    step = scale * correction[...] + gain * remaining
    moved = multipliers[...] + step
    new_multipliers[...] = moved
    both = dot(modes[...], side_by_side(moved))
    coeffs[...] = fold(both[:NM] + both[NM:])


def last_step(
    scale, gain, scalars, modes, product, weight, residual, correction, multipliers, received
):
    return pl.pallas_call(
        functools.partial(last_kernel, scale, gain),
        out_shape=[VEC, COEF],
        in_specs=[SMEM] + [VMEM] * 12,
        out_specs=[VMEM] * 2,
        scratch_shapes=[pltpu.VMEM((M + PCAP, LOADS), f32)],
        compiler_params=params(8),
        name="last",
    )(scalars, modes, product, weight, residual, correction, multipliers, *received)


def join_kernel(*refs):
    out = refs[-1]
    for k, ref in enumerate(refs[:-1]):
        out[pl.ds(k * NM, NM), :] = ref[...]


def join(pieces):
    return pl.pallas_call(
        join_kernel,
        out_shape=jax.ShapeDtypeStruct((len(pieces) * NM, LOADS), f32),
        in_specs=[VMEM] * len(pieces),
        out_specs=VMEM,
        compiler_params=params(4),
        name="join",
    )(*pieces)


def blocks_kernel(*refs):
    out = refs[-1]
    for mask, block in enumerate(refs[:-1]):
        high, low = split(block[...])
        out[pl.ds(mask * NM, NM), :] = high
        out[pl.ds((8 + mask) * NM, NM), :] = low


def prepare_blocks(blocks):
    return pl.pallas_call(
        blocks_kernel,
        out_shape=jax.ShapeDtypeStruct((16 * NM, 16 * NM), bf16),
        in_specs=[VMEM] * 8,
        out_specs=VMEM,
        compiler_params=params(8),
        name="blocks",
    )(*blocks)


def coarse_kernel(scalars, blocks, *rest):
    gathered, parts, scratch = rest[:4], rest[4:6], rest[6]
    for group in range(4):
        for item in range(4):
            slot = scalars[12 + group * 4 + item]
            rows = pl.ds(pl.multiple_of(slot * NM, NM), NM)
            scratch[rows, :] = side_by_side(gathered[group][pl.ds(item * NM, NM), :])
    half = 8 * NM
    both = dot(blocks[pl.ds(0, half), :], scratch[...])
    both = fold(both + dot(blocks[pl.ds(half, half), :], scratch[...]))
    parts[0][...] = both[: 4 * NM]
    parts[1][...] = both[4 * NM :]


def coarse_product(scalars, blocks, gathered):
    return pl.pallas_call(
        coarse_kernel,
        out_shape=[jax.ShapeDtypeStruct((4 * NM, LOADS), f32)] * 2,
        in_specs=[SMEM] + [VMEM] * 5,
        out_specs=[VMEM] * 2,
        scratch_shapes=[pltpu.VMEM((16 * NM, 2 * LOADS), bf16)],
        compiler_params=params(8),
        name="coarse",
    )(scalars, blocks, *gathered)


def sum_kernel(kept, partner, *parts):
    for k, part in enumerate(parts):
        rows = pl.ds(k * NM, NM)
        part[...] = kept[rows, :] + partner[rows, :]


def sum_parts(kept, partner):
    return pl.pallas_call(
        sum_kernel,
        out_shape=[COEF] * 4,
        in_specs=[VMEM] * 2,
        out_specs=[VMEM] * 4,
        compiler_params=params(4),
        name="sum",
    )(kept, partner)


def apply_kernel(high, low, vectors, product, wide):
    wide[...] = side_by_side(vectors[...])

    def chunk(k, carry):
        rows = pl.ds(pl.multiple_of(k * WIDE_CHUNK, WIDE_CHUNK), WIDE_CHUNK)
        product[rows, :] = fold(dot(high[rows, :], wide[...]) + dot(low[rows, :], wide[...]))
        return carry

    lax.fori_loop(0, M // WIDE_CHUNK, chunk, 0)


def apply_alone(high, low, vectors):
    return pl.pallas_call(
        apply_kernel,
        out_shape=VEC,
        in_specs=[VMEM] * 3,
        out_specs=VMEM,
        scratch_shapes=OPERATOR_SCRATCH[:1],
        compiler_params=params(8),
        name="apply",
    )(high, low, vectors)


def project_kernel(scalars, modes_t, applied_modes, applied, multipliers, *rest):
    parts, (new_multipliers, product), pieces = rest[:4], rest[4:6], rest[6:12]
    amplitude = (parts[0][...] + parts[1][...]) + (parts[2][...] + parts[3][...])
    amp_high, amp_low = split(amplitude)
    stacked = jnp.concatenate([amp_high, amp_high, amp_low], axis=0)
    both = jnp.concatenate([amp_high, amp_low], axis=1)
    modes_high, modes_low = split(applied_modes[:, pl.ds(0, NM)])
    removed = fold(dot(modes_high, both)) + dot(modes_low, amp_high)
    product[pl.ds(0, M), :] = applied[...] - removed
    product[pl.ds(M, PCAP), :] = jnp.zeros((PCAP, LOADS), f32)
    cut(scalars, product, pieces)
    new_multipliers[...] = multipliers[...] - dot(modes_t[...], stacked)


def project_step(scalars, modes_t, applied_modes, applied, multipliers, parts):
    return pl.pallas_call(
        project_kernel,
        out_shape=[VEC, PADDED] + [PIECE] * 6,
        in_specs=[SMEM] + [VMEM] * 8,
        out_specs=[VMEM] * 8,
        compiler_params=params(8),
        name="project",
    )(scalars, modes_t, applied_modes, applied, multipliers, *parts)


def emit_kernel(vectors, out):
    out[...] = vectors[...].T


def emit(vectors):
    return pl.pallas_call(
        emit_kernel,
        out_shape=jax.ShapeDtypeStruct((LOADS, M), f32),
        in_specs=[VMEM],
        out_specs=VMEM,
        compiler_params=params(8),
        name="emit",
    )(vectors)


def final_kernel(scalars, product, weight, data, *rest):
    received, (residual_out, padded) = rest[:6], rest[6:]
    applied = place(scalars, product, received, padded) * weight[...]
    residual_out[...] = (data[...] - applied).T


def final_step(scalars, product, weight, data, received):
    return pl.pallas_call(
        final_kernel,
        out_shape=jax.ShapeDtypeStruct((LOADS, M), f32),
        in_specs=[SMEM] + [VMEM] * 9,
        out_specs=VMEM,
        scratch_shapes=[pltpu.VMEM((M + PCAP, LOADS), f32)],
        compiler_params=params(8),
        name="final",
    )(scalars, product, weight, data, *received)


def swap_pairs(count, odd):
    lower = range(odd, count, 2)
    pairs = [(i, (i + 1) % count) for i in lower]
    return pairs + [(target, source) for source, target in pairs]


def exchange(pieces):
    received = []
    for piece, (number, kind) in zip(pieces, SLOTS):
        axes = (GX, GY, GZ)[number]
        received.append(lax.ppermute(piece, axes, swap_pairs(lax.axis_size(axes), kind)))
    return received


def xor_pairs(count, mask):
    return [(i, i ^ mask) for i in range(count)]


def per_device(
    load_data,
    initial_dual,
    dual_operator,
    coarse_modes,
    coarse_inverse,
    face_start,
    face_len,
    multiplicity,
):
    def gather(coeffs):
        line = join(
            [coeffs]
            + [lax.ppermute(coeffs, ("xh", "xl"), xor_pairs(4, mask)) for mask in range(1, 4)]
        )
        return [line] + [lax.ppermute(line, "y", xor_pairs(4, mask)) for mask in range(1, 4)]

    def scatter(kept, sent, beside):
        parts = sum_parts(kept, lax.ppermute(sent, "co", xor_pairs(2, 1)))
        parts = [parts[0]] + [
            lax.ppermute(parts[mask], "gy", xor_pairs(4, mask)) for mask in range(1, 4)
        ]
        return lax.optimization_barrier((parts, beside))

    high, low, multipliers, product, *pieces, scalars, start_gains, inner_gains = first_apply(
        face_start[0, 0, 0], face_len[0, 0, 0], dual_operator[0, 0, 0], initial_dual[0, 0, 0]
    )
    data, weight, modes_rows, modes_t, modes_wide, *blocks = turn(
        scalars, load_data[0, 0, 0], multiplicity[0, 0], coarse_modes[0, 0, 0], coarse_inverse
    )

    def move_blocks(received, masks):
        for mask in masks:
            blocks[mask] = lax.ppermute(blocks[mask], RSG, xor_pairs(8, mask))
        moved = [blocks[mask] for mask in masks]
        received, moved = lax.optimization_barrier((received, moved))
        for mask, block in zip(masks, moved):
            blocks[mask] = block
        return received

    received = exchange(pieces)
    for outer in range(OUTER):
        residual = correction = data
        for index in range(CHEB - 1):
            if outer == 0:
                received = move_blocks(received, WINDOWS[index])
            residual, correction, multipliers, product, *pieces = step(
                scalars, inner_gains if index else start_gains, high, low, product, weight,
                residual, correction, multipliers, received,
            )
            if outer == 0 and index == 0:
                modes_wide, residual = lax.optimization_barrier((modes_wide, residual))
                applied_modes = apply_alone(high, low, modes_wide)
            received = exchange(pieces)
        if outer == 0:
            received = move_blocks(received, WINDOWS[-1])
            for mask in (1, 3):
                blocks[mask] = lax.ppermute(blocks[mask], RSG, xor_pairs(8, mask))
            prepared = prepare_blocks(blocks)
        multipliers, coeffs = last_step(
            *GAINS[-1], scalars, modes_rows, product, weight,
            residual, correction, multipliers, received,
        )
        applied = apply_alone(high, low, multipliers)
        gathered, applied = lax.optimization_barrier((gather(coeffs), applied))
        parts, applied_modes = scatter(
            *coarse_product(scalars, prepared, gathered), applied_modes
        )
        multipliers, product, *pieces = project_step(
            scalars, modes_t, applied_modes, applied, multipliers, parts
        )
        received = exchange(pieces)
    solved = emit(multipliers)
    final_residual = final_step(scalars, product, weight, data, received)
    return solved.reshape(initial_dual.shape), final_residual.reshape(initial_dual.shape)


def solution(mesh):
    fine = Mesh(mesh.devices.reshape(2, 2, 4, 4, 2), ("xh", "co", "gy", "y", "xl"))
    grid = (GX, "gy", GZ)
    placed = (
        P(*grid, None, None),
        P(*grid, None, None),
        P(*grid, None, None),
        P(*grid, None, None),
        P(("xh", "co", "gy", "y", "xl"), None),
        P(*grid, None),
        P(*grid, None),
        P(*grid, None),
    )
    return jax.shard_map(
        per_device,
        mesh=fine,
        in_specs=placed,
        out_specs=(P(*grid, None, None), P(*grid, None, None)),
        check_vma=False,
    )
```
